256 devices in a mesh: ctx: 32 (over z, x), head: 8 (over y, core).
Axes of the slice: x: 4, y: 4, z: 8, core: 2. Of those that a mesh axis runs over, the one named last changes fastest.
Arguments:
- queries: bfloat16 [65536, 2048], P('ctx', 'head'), may hold values from -6 to 6
- keys: bfloat16 [65536, 2048], P('ctx', 'head'), may hold values from -6 to 6
- values: bfloat16 [65536, 4096], P('ctx', 'head'), may hold values from -6 to 6
- gate_pre: float32 [2, 8, 65536], P(None, None, ('ctx', 'head')), may hold values from -8 to 320
Outputs:
- hidden: bfloat16 [65536, 4096], P('ctx', 'head')
- closing_memory: float32 [8, 256, 512], P('head', 'ctx')
- final_norm: float32 [8, 256], P('head')
- final_max: float32 [8], P('head')
The draws below stay inside these ranges and needn't reach their ends.
All inputs are finite; a program needn't handle non-finite values.
Results may differ from the reference program's by a relative error of at most 0.004.
Values sent between devices are 32-bit elements; how exact they have to be, the bound alone decides.
No kernel may reach another device: no remote copies, remote signals or barrier semaphores. Data moves between devices by JAX's collectives and lax.ppermute only.
A program may use at most 64 MiB of HBM per device.

```python
import jax
import jax.numpy as jnp
from jax import lax

HEAD_COUNT = 8
DQK = 256
DV = 512
TOK_DEV = 2048
BLK = 512
PROMPT_TOKENS = 65536


def draw_gate_pre(key, part):
    keys = jax.random.split(jax.random.fold_in(key, 17), 10)
    row_entries = jnp.arange(HEAD_COUNT)[:, None]
    base = jnp.clip(1.5 * jax.random.normal(keys[0], (HEAD_COUNT, PROMPT_TOKENS), jnp.float32), -8.0, 8.0)
    base = base.at[:, 1].set(-8.0)
    share = 0.5
    fast = jax.random.bernoulli(keys[4], share, (HEAD_COUNT,))
    fast_rate = jax.random.uniform(keys[5], (HEAD_COUNT,), jnp.float32, 1.0 / 50.0, 1.0 / 30.0)
    rate = jnp.where(fast, fast_rate, 0.5 / PROMPT_TOKENS)
    regions = jnp.exp(jax.random.uniform(keys[6], (HEAD_COUNT, PROMPT_TOKENS // TOK_DEV), jnp.float32, -0.7, 0.7))
    regions = jnp.repeat(regions, TOK_DEV, axis=1)
    rough = jnp.exp(jax.random.uniform(keys[7], (HEAD_COUNT, PROMPT_TOKENS), jnp.float32, -0.7, 0.7))
    forget_decay = rate[:, None] * regions * rough
    spike_position = jax.random.randint(keys[8], (HEAD_COUNT, 3), 0, PROMPT_TOKENS)
    spike_input = jax.random.uniform(keys[9], (HEAD_COUNT, 3), jnp.float32, 0.22, 0.51)
    forget_decay = forget_decay.at[row_entries, spike_position].set(spike_input)
    forget = -jnp.log(jnp.expm1(forget_decay))
    return jnp.stack([base, forget], axis=0).astype(jnp.float32)


def block_levels(stream_key, shape, cuts, smallest, largest):
    level = 1.0
    for dim, blocks in cuts:
        draws = jax.random.uniform(jax.random.fold_in(jax.random.fold_in(stream_key, 6), dim), (blocks,), jnp.float32, smallest / len(cuts), largest / len(cuts))
        level = level * jnp.repeat(jnp.exp(draws), shape[dim] // blocks).reshape((-1,) + (1,) * (len(shape) - 1 - dim))
    return level


def scatter_about(own_key, shape, spread, most, shards=(), kind=jnp.bfloat16):
    loudness = block_levels(own_key, shape, shards, -0.22, 0.18) if shards else 1.0
    values = jax.random.normal(own_key, shape, jnp.float32) * spread * loudness
    return jnp.minimum(jnp.maximum(values, -most), most).astype(kind)


def setup_inputs(seed: int = 0) -> dict:
    key_of = jax.random.split(jax.random.key(seed), 5)
    queries = scatter_about(key_of[0], (PROMPT_TOKENS, HEAD_COUNT * DQK), 1.0, 6.0, ((0, 32), (1, 8)))
    keys = scatter_about(key_of[1], (PROMPT_TOKENS, HEAD_COUNT * DQK), 1.0, 6.0, ((0, 32), (1, 8)))
    values = scatter_about(key_of[2], (PROMPT_TOKENS, HEAD_COUNT * DV), 1.0, 6.0, ((0, 32), (1, 8)))
    gate_pre = draw_gate_pre(jax.random.fold_in(key_of[4], 71), 0)
    return {"queries": queries, "keys": keys, "values": values, "gate_pre": gate_pre}


NEG = -1.0e30


def block_step(carry, inputs):
    memory, normal, stab, offset = carry
    q_block, key_block, v_block, in_gate, forget = inputs
    length = q_block.shape[0]
    scale = q_block.shape[1] ** -0.5
    log_forget = jax.nn.log_sigmoid(forget)
    cum = jnp.cumsum(log_forget)
    whole = cum[-1]
    places = jnp.arange(length, dtype=jnp.int32)
    causal = places[:, None] >= places[None, :]
    log_weight = jnp.where(causal, cum[:, None] - cum[None, :] + in_gate[None, :], NEG)
    top = jnp.maximum(cum + stab, jnp.max(log_weight, axis=1))
    weights = jnp.where(causal, jnp.exp(log_weight - top[:, None]), 0.0)
    scores = jnp.dot(q_block, key_block.T, preferred_element_type=jnp.float32) * scale
    mixed = weights * scores
    denom = jnp.sum(mixed, axis=1)
    numer = jnp.dot(mixed.astype(jnp.bfloat16), v_block, preferred_element_type=jnp.float32)
    carried = jnp.exp(cum + stab - top)
    q_float = q_block.astype(jnp.float32)
    numer = numer + carried[:, None] * jnp.dot(q_float, memory, precision=lax.Precision.HIGHEST)
    denom = denom + carried * jnp.dot(q_float, normal, precision=lax.Precision.HIGHEST)
    new_stab = jnp.maximum(whole + stab, jnp.max(whole - cum + in_gate))
    keep = jnp.exp(whole + stab - new_stab)
    taken = jnp.exp(whole - cum + in_gate - new_stab)
    k_float = key_block.astype(jnp.float32) * scale * taken[:, None]
    memory = keep * memory + jnp.dot(k_float.T, v_block.astype(jnp.float32), precision=lax.Precision.HIGHEST)
    normal = keep * normal + jnp.sum(k_float, axis=0)
    return (memory, normal, new_stab, offset + whole), (numer, denom, top, cum + offset)


def one_head(args):
    q_head, k_head, v_head, in_gate, forget = args
    count = q_head.shape[0] // BLK
    blocks = (q_head.reshape(count, BLK, DQK), k_head.reshape(count, BLK, DQK),
              v_head.reshape(count, BLK, DV), in_gate.reshape(count, BLK), forget.reshape(count, BLK))
    start = (jnp.zeros((DQK, DV), jnp.float32), jnp.zeros((DQK,), jnp.float32),
             jnp.full((), NEG, jnp.float32), jnp.zeros((), jnp.float32))
    final, outs = lax.scan(block_step, start, blocks)
    numer, denom, top, cum = outs
    result = numer / jnp.maximum(jnp.abs(denom), 1.0)[..., None]
    return result.reshape(q_head.shape[0], DV).astype(jnp.bfloat16), final[0], final[1], final[2]


def reference(queries, keys, values, gate_pre):
    q_heads = queries.reshape(PROMPT_TOKENS, HEAD_COUNT, DQK).transpose(1, 0, 2)
    k_heads = keys.reshape(PROMPT_TOKENS, HEAD_COUNT, DQK).transpose(1, 0, 2)
    v_heads = values.reshape(PROMPT_TOKENS, HEAD_COUNT, DV).transpose(1, 0, 2)
    hidden, memory, normal, stab = lax.map(one_head, (q_heads, k_heads, v_heads, gate_pre[0], gate_pre[1]))
    hidden = hidden.transpose(1, 0, 2).reshape(PROMPT_TOKENS, HEAD_COUNT * DV)
    return hidden, memory, normal, stab
```

```python
import functools

import jax
import jax.numpy as jnp
from jax import lax
from jax.experimental import pallas as pl
from jax.experimental.pallas import tpu as pltpu
from jax.sharding import Mesh
from jax.sharding import PartitionSpec as P

DQK = 256
DV = 512
XS = 4
ZS = 8
ROWS = DQK // (XS * ZS)
SLICE = ZS * ROWS
SENT = SLICE + 8
PIECES = 8
PIECE = 256
LANES = 128
WIDE = DV + LANES
TOKS = PIECES * PIECE
QB = 512
BLOCKS = TOKS // QB
PARTS = ((3,), (2,), (0, 1))
CTX = ("ctx_0", "ctx_1")
CTX_HEAD = ("ctx_0", "ctx_1", "head")
NEG = -1e30
F32 = jnp.float32
BF16 = jnp.bfloat16
VMEM = pl.BlockSpec(memory_space=pltpu.VMEM)
SMEM = pl.BlockSpec(memory_space=pltpu.SMEM)
HBM = pl.BlockSpec(memory_space=pltpu.HBM)
ANY = pl.BlockSpec(memory_space=pl.ANY)
MIB = 1 << 20


def in_hbm(x):
    return pltpu.with_memory_space_constraint(x, pltpu.HBM)


def log_sigmoid(x):
    z = jnp.exp(-jnp.abs(x))
    s = z / (2.0 + z)
    s2 = s * s
    tail = jnp.full_like(s, 1.0 / 17.0)
    for n in (15, 13, 11, 9, 7, 5, 3, 1):
        tail = tail * s2 + 1.0 / n
    return jnp.minimum(x, 0.0) - 2.0 * s * tail


def three_parts(x):
    high = x.astype(BF16)
    rest = x - high.astype(F32)
    mid = rest.astype(BF16)
    low = (rest - mid.astype(F32)).astype(BF16)
    return high, mid, low


def piece_sums(forget):
    n = forget.shape[1]
    upto = lax.broadcasted_iota(jnp.int32, (n, n), 0) <= lax.broadcasted_iota(jnp.int32, (n, n), 1)
    ones = jnp.where(upto, 1.0, 0.0).astype(BF16)
    parts = jnp.concatenate([p.astype(F32) for p in three_parts(log_sigmoid(forget))], axis=0)
    sums = jnp.dot(parts.astype(BF16), ones, preferred_element_type=F32)
    k = forget.shape[0]
    return sums[:k] + sums[k : 2 * k] + sums[2 * k :]


def gate_kernel(g_ref, out_ref):
    cum = piece_sums(g_ref[1])
    own = g_ref[0] - cum
    for h in range(own.shape[0]):
        out_ref[h, 0:1, :] = own[h : h + 1]
        out_ref[h, 1:2, :] = cum[h : h + 1]


def gate_sums(gate_pre):
    kinds, heads, n = gate_pre.shape
    return pl.pallas_call(
        gate_kernel,
        in_specs=[VMEM],
        out_specs=VMEM,
        out_shape=pltpu.VMEM((heads, kinds, n), F32),
        compiler_params=pltpu.CompilerParams(vmem_limit_bytes=8 * MIB),
        name="gate_sums",
    )(gate_pre)


def turned_kernel(k_ref, kt_ref):
    kt_ref[...] = k_ref[...].T


def turned(keys):
    return pl.pallas_call(
        turned_kernel,
        grid=(4,),
        in_specs=[pl.BlockSpec((TOKS // 4, DQK), lambda i: (i, 0))],
        out_specs=pl.BlockSpec((DQK, TOKS // 4), lambda i: (0, i)),
        out_shape=jax.ShapeDtypeStruct((DQK, TOKS), BF16),
        compiler_params=pltpu.CompilerParams(vmem_limit_bytes=8 * MIB),
        cost_estimate=pl.CostEstimate(flops=0, bytes_accessed=4 * MIB, transcendentals=0),
        name="turn_keys",
    )(keys)


def state_kernel(x_ref, g_ref, kt_ref, v_hbm, own_ref, one_ref, two_ref, three_ref, tick_ref, v_ref, w_ref, acc_ref, sem):
    copies = []
    for j in range(BLOCKS):
        span = pl.ds(j * QB, QB)
        copies.append(pltpu.make_async_copy(v_hbm.at[span], v_ref.at[span], sem.at[j]))
        copies[-1].start()
    own = g_ref[:, 0, :]
    cum = g_ref[:, 1, :]
    later = jnp.broadcast_to(cum[:, PIECE - 1 :], cum.shape)
    row = lax.broadcasted_iota(jnp.int32, cum.shape, 0)
    for shift in (1, 2, 4):
        moved = pltpu.roll(later, PIECES - shift, 0)
        later = later + jnp.where(row + shift < PIECES, moved, 0.0)
    reach = own + later
    stab = jnp.max(jnp.max(reach, axis=1, keepdims=True), axis=0, keepdims=True)
    w_ref[...] = jnp.exp(reach - stab) * (DQK**-0.5)
    norm = jnp.zeros((24, DQK), F32)
    for j in range(BLOCKS):
        span = pl.ds(j * QB, QB)
        weight = jnp.concatenate([w_ref[2 * j : 2 * j + 1, :], w_ref[2 * j + 1 : 2 * j + 2, :]], axis=1)
        k = kt_ref[:, span]
        scaled = (k.astype(F32) * weight).astype(BF16)
        parts = [jnp.broadcast_to(p.astype(F32), (8, QB)) for p in three_parts(weight)]
        parts = jnp.concatenate(parts, axis=0).astype(BF16)
        norm += lax.dot_general(parts, k, (((1,), (1,)), ((), ())), preferred_element_type=F32)
        copies[j].wait()
        product = jnp.dot(scaled, v_ref[span, :], preferred_element_type=F32)
        if j:
            product += acc_ref[...].reshape(DQK, DV)
        acc_ref[...] = product.reshape(ZS, XS, ROWS, DV)
    norm = norm[0:8] + norm[8:16] + norm[16:24]
    row = lax.broadcasted_iota(jnp.int32, (8, DV), 0)
    extra = jnp.concatenate([norm, norm], axis=1)
    extra = jnp.where(row == 1, stab, extra)
    extra = jnp.where(row == 2, later[0:1, 0:1], extra)
    x = x_ref[0]
    for k, ref in enumerate((own_ref, one_ref, two_ref, three_ref)):
        to = lax.rem(x + k, XS)
        ref[0:SLICE, :] = acc_ref[:, pl.ds(to, 1)].reshape(SLICE, DV)
        ref[SLICE:, :] = extra
    tick_ref[...] = extra[:, :LANES]


def state(x, gates, keys_t, values):
    return pl.pallas_call(
        state_kernel,
        in_specs=[SMEM, VMEM, VMEM, HBM],
        out_specs=[VMEM] * 5,
        out_shape=[pltpu.VMEM((SENT, DV), F32)] * 4 + [pltpu.VMEM((8, LANES), F32)],
        scratch_shapes=[
            pltpu.VMEM((TOKS, DV), BF16),
            pltpu.VMEM((PIECES, PIECE), F32),
            pltpu.VMEM((ZS, XS, ROWS, DV), F32),
            pltpu.SemaphoreType.DMA((BLOCKS,)),
        ],
        compiler_params=pltpu.CompilerParams(vmem_limit_bytes=12 * MIB),
        cost_estimate=pl.CostEstimate(flops=600_000_000, bytes_accessed=5 * MIB, transcendentals=0),
        name="shard_state",
    )(x, gates, keys_t, values)


def wide(x, n):
    return jnp.concatenate([x] * (n // LANES), axis=1)


def group_kernel(x_ref, own_ref, one_ref, two_ref, three_ref, after_ref, out_ref, all_ref, small_ref):
    x = x_ref[0]
    row = lax.broadcasted_iota(jnp.int32, (8, LANES), 0)
    for k, ref in enumerate((own_ref, one_ref, two_ref, three_ref)):
        at = lax.rem(x + XS - k, XS)
        all_ref[pl.ds(at, 1)] = ref[0:SLICE, :].reshape(1, ZS, ROWS, DV)
        tail = ref[SLICE:, :]
        small = jnp.where(row == 0, tail[0:1, :LANES], tail[0:1, LANES : 2 * LANES])
        small = jnp.where(row == 2, tail[1:2, :LANES], small)
        small = jnp.where(row == 3, tail[2:3, :LANES], small)
        small_ref[pl.ds(at, 1)] = small.reshape(1, 8, LANES)
    stab = small_ref[0, 2:3, :]
    total = small_ref[0, 3:4, :]
    normal = small_ref[0]
    keeps, takes = [], []
    for j in range(1, XS):
        own_total = small_ref[j, 3:4, :]
        own_stab = small_ref[j, 2:3, :]
        shifted = stab + own_total
        stab = jnp.maximum(shifted, own_stab)
        total = total + own_total
        keep, take = jnp.exp(shifted - stab), jnp.exp(own_stab - stab)
        normal = keep * normal + take * small_ref[j]
        keeps.append(wide(keep, DV))
        takes.append(wide(take, DV))
    for z in range(ZS):
        memory = all_ref[0, z]
        for j in range(1, XS):
            memory = keeps[j - 1] * memory + takes[j - 1] * all_ref[j, z]
        out_ref[z, :, :DV] = memory
    extra = jnp.where(row == 2, stab, normal)
    extra = jnp.where(row == 3, total, extra)
    out_ref[:, :, DV:] = jnp.broadcast_to(extra[None], (ZS, 8, LANES))


def grouped(x, parts, after):
    return pl.pallas_call(
        group_kernel,
        in_specs=[SMEM] + [VMEM] * 4 + [HBM],
        out_specs=[VMEM] * 3,
        out_shape=[
            pltpu.VMEM((ZS, ROWS, WIDE), F32),
            pltpu.HBM((XS, ZS, ROWS, DV), F32),
            pltpu.VMEM((XS, 8, LANES), F32),
        ],
        compiler_params=pltpu.CompilerParams(vmem_limit_bytes=4 * MIB),
        cost_estimate=pl.CostEstimate(flops=1_000_000, bytes_accessed=2 * MIB, transcendentals=0),
        name="group_states",
    )(x, *parts, in_hbm(after))


def chain_kernel(x_ref, z_ref, got_ref, small_ref, after_ref, before_ref, close_ref, norm_ref, top_ref, group_ref, mine_ref):
    row = lax.broadcasted_iota(jnp.int32, (8, LANES), 0)
    stab = jnp.full((1, LANES), NEG, F32)
    memory = jnp.zeros((ROWS, DV), F32)
    normal = jnp.zeros((8, LANES), F32)
    group = normal
    for k in range(ZS):
        before_ref[k] = memory
        group = jnp.where(z_ref[0] == k, jnp.where(row == 2, stab, normal), group)
        shifted = stab + got_ref[k, 3:4, DV:]
        own_stab = got_ref[k, 2:3, DV:]
        stab = jnp.maximum(shifted, own_stab)
        keep, take = jnp.exp(shifted - stab), jnp.exp(own_stab - stab)
        memory = wide(keep, DV) * memory + wide(take, DV) * got_ref[k, :, :DV]
        normal = keep * normal + take * got_ref[k, :, DV:]
    close_ref[0] = memory
    norm_ref[0:1, :LANES] = normal[0:1]
    norm_ref[0:1, LANES:] = normal[1:2]
    top_ref[...] = stab
    group_ref[...] = group
    mine = group
    normal, stab = group, group[2:3]
    for j in range(XS - 1):
        shifted = stab + small_ref[j, 3:4, :]
        own_stab = small_ref[j, 2:3, :]
        stab = jnp.maximum(shifted, own_stab)
        keep, take = jnp.exp(shifted - stab), jnp.exp(own_stab - stab)
        normal = keep * normal + take * small_ref[j]
        mine = jnp.where(x_ref[0] == j + 1, jnp.where(row == 2, stab, normal), mine)
    mine_ref[...] = mine


def chained(x, z, got, small, after):
    return pl.pallas_call(
        chain_kernel,
        in_specs=[SMEM, SMEM, VMEM, VMEM, HBM],
        out_specs=[VMEM] * 6,
        out_shape=[
            pltpu.VMEM((ZS, ROWS, DV), F32),
            pltpu.HBM((1, ROWS, DV), F32),
            pltpu.HBM((1, DQK), F32),
            pltpu.HBM((1, LANES), F32),
            pltpu.VMEM((8, LANES), F32),
            pltpu.VMEM((8, LANES), F32),
        ],
        compiler_params=pltpu.CompilerParams(vmem_limit_bytes=4 * MIB),
        cost_estimate=pl.CostEstimate(flops=1_000_000, bytes_accessed=MIB, transcendentals=0),
        name="chain_groups",
    )(x, z, got, small, in_hbm(after))


def spread_kernel(x_ref, got_ref, all_ref, small_ref, group_ref, mine_in, own_ref, one_ref, two_ref, three_ref, mine_ref, out_ref):
    x = x_ref[0]
    stab = group_ref[2:3, :]
    keeps, takes = [], []
    for j in range(XS - 1):
        shifted = stab + small_ref[j, 3:4, :]
        own_stab = small_ref[j, 2:3, :]
        stab = jnp.maximum(shifted, own_stab)
        keeps.append(wide(jnp.exp(shifted - stab), DV))
        takes.append(wide(jnp.exp(own_stab - stab), DV))
    for z in range(ZS):
        memory = got_ref[z]
        out_ref[0, z] = memory
        for j in range(XS - 1):
            memory = keeps[j] * memory + takes[j] * all_ref[j, z]
            out_ref[j + 1, z] = memory
    for k, ref in enumerate((own_ref, one_ref, two_ref, three_ref)):
        to = lax.rem(x + k, XS)
        ref[...] = out_ref[pl.ds(to, 1)].reshape(ZS, ROWS, DV)
    mine_ref[...] = mine_in[...]


def spread(x, got, everything, small, group, mine):
    return pl.pallas_call(
        spread_kernel,
        in_specs=[SMEM] + [VMEM] * 5,
        out_specs=[VMEM] * 5,
        out_shape=[pltpu.VMEM((ZS, ROWS, DV), F32)] * 4 + [pltpu.VMEM((8, LANES), F32)],
        scratch_shapes=[pltpu.VMEM((XS, ZS, ROWS, DV), F32)],
        compiler_params=pltpu.CompilerParams(vmem_limit_bytes=4 * MIB),
        cost_estimate=pl.CostEstimate(flops=1_000_000, bytes_accessed=2 * MIB, transcendentals=0),
        name="spread_prefixes",
    )(x, got, everything, small, group, mine)


def column(row):
    n = row.shape[1]
    return jnp.concatenate(
        [
            jnp.broadcast_to(row[:, at : at + LANES], (LANES, LANES)).T
            for at in range(0, n, LANES)
        ],
        axis=0,
    )


def tables(g_ref, table_ref):
    own, cum = [], []
    for r in range(0, PIECES, 2):
        first = g_ref[r, 1:2, :][:, PIECE - 1 :]
        own.append(jnp.concatenate([g_ref[r, 0:1, :], g_ref[r + 1, 0:1, :] - first], axis=1))
        cum.append(jnp.concatenate([g_ref[r, 1:2, :], g_ref[r + 1, 1:2, :] + first], axis=1))
    own = jnp.concatenate(own, axis=0)
    cum = jnp.concatenate(cum, axis=0)
    table_ref[0:BLOCKS, :] = own
    table_ref[BLOCKS : 2 * BLOCKS, :] = cum
    lane = lax.broadcasted_iota(jnp.int32, (BLOCKS, QB), 1)
    top = own
    shift = 1
    while shift < QB:
        moved = pltpu.roll(top, shift, 1)
        top = jnp.maximum(top, jnp.where(lane >= shift, moved, NEG))
        shift *= 2
    stab = jnp.full((1, 1), NEG, F32)
    for r in range(BLOCKS):
        at = 2 * BLOCKS + r
        table_ref[at : at + 1, :] = jnp.maximum(top[r : r + 1], stab)
        stab = jnp.maximum(stab, top[r : r + 1, QB - 1 :]) + cum[r : r + 1, QB - 1 :]


def attend(blocks, hbm, num_hbm, den_hbm, num_ref, den_ref, table_ref, q_ref, k_ref, v_ref, in_sem, out_sem, ready):
    q_hbm, k_hbm, v_hbm = hbm
    last = blocks[-1]

    def fetch(n, ref, j):
        span = pl.ds(pl.multiple_of(j * QB, QB), QB)
        return pltpu.make_async_copy(hbm[n].at[span], ref.at[span], in_sem.at[n, j])

    for i in reversed(blocks):
        fetch(0, q_ref, i).start()
    for j in range(last, -1, -1):
        fetch(1, k_ref, j).start()
        fetch(2, v_ref, j).start()
    ready()
    copies = []
    for n in range(len(blocks) - 1, -1, -1):
        i = blocks[n]
        here = pl.ds(n * QB, QB)
        top = wide(column(table_ref[2 * BLOCKS + i : 2 * BLOCKS + i + 1, :]), QB)
        fetch(0, q_ref, i).wait()
        q = q_ref[pl.ds(i * QB, QB), :]
        fresh = n == len(blocks) - 1

        def block(j, shift, masked):
            if fresh:
                fetch(1, k_ref, j).wait()
            at = pl.ds(pl.multiple_of(j * QB, QB), QB)
            scores = lax.dot_general(q, k_ref[at, :], (((1,), (1,)), ((), ())), preferred_element_type=F32) * (DQK**-0.5)
            power = (table_ref[pl.ds(j, 1), :] + shift) - top
            if masked:
                past = lax.broadcasted_iota(jnp.int32, (QB, QB), 0) >= lax.broadcasted_iota(jnp.int32, (QB, QB), 1)
                power = jnp.where(past, power, NEG)
            mixed = jnp.exp(power) * scores
            if fresh:
                fetch(2, v_ref, j).wait()
            lanes = sum(mixed[:, c : c + LANES] for c in range(0, QB, LANES))
            return lanes, jnp.dot(mixed.astype(BF16), v_ref[at, :], preferred_element_type=F32)

        den_ref[here, :], num_ref[here, :] = block(i, jnp.zeros((1, 1), F32), True)

        def earlier(m, shift):
            j = i - 1 - m
            shift = shift + table_ref[pl.ds(BLOCKS + j, 1), :][:, QB - 1 :]
            lanes, product = block(j, shift, False)
            den_ref[here, :] += lanes
            num_ref[here, :] += product
            return shift

        if i:
            lax.fori_loop(0, i, earlier, jnp.zeros((1, 1), F32))
        for m, (ref, out) in enumerate(((num_ref, num_hbm), (den_ref, den_hbm))):
            copies.append(pltpu.make_async_copy(ref.at[here], out.at[here], out_sem.at[m, n]))
            copies[-1].start()
    for copy in copies:
        copy.wait()


def first_kernel(blocks, g_ref, tick_ref, q_hbm, k_hbm, v_hbm, num_hbm, den_hbm, table_hbm, num_ref, den_ref, table_ref, q_ref, k_ref, v_ref, in_sem, out_sem, sem):
    copy = pltpu.make_async_copy(table_ref, table_hbm, sem)

    def ready():
        tables(g_ref, table_ref)
        copy.start()

    attend(blocks, (q_hbm, k_hbm, v_hbm), num_hbm, den_hbm, num_ref, den_ref, table_ref, q_ref, k_ref, v_ref, in_sem, out_sem, ready)
    copy.wait()


def next_kernel(blocks, table_hbm, tick_ref, q_hbm, k_hbm, v_hbm, num_hbm, den_hbm, num_ref, den_ref, table_ref, q_ref, k_ref, v_ref, in_sem, out_sem, sem):
    copy = pltpu.make_async_copy(table_hbm, table_ref, sem)
    copy.start()
    attend(blocks, (q_hbm, k_hbm, v_hbm), num_hbm, den_hbm, num_ref, den_ref, table_ref, q_ref, k_ref, v_ref, in_sem, out_sem, copy.wait)


def last_kernel(blocks, table_hbm, tick_ref, q_hbm, k_hbm, v_hbm, all_hbm, num_hbm, den_hbm, all_ref, *rest):
    sem = rest[-1]
    copy = pltpu.make_async_copy(all_hbm, all_ref, sem)
    next_kernel(blocks, table_hbm, tick_ref, q_hbm, k_hbm, v_hbm, num_hbm, den_hbm, *rest[:-1])
    copy.start()
    copy.wait()


def local(blocks, gates, tick, queries, keys, values, table=None, everything=None):
    count = len(blocks)
    units = sum(blocks) + count
    args = [gates if table is None else in_hbm(table), tick, in_hbm(queries), in_hbm(keys), in_hbm(values)]
    in_specs = [VMEM if table is None else HBM, ANY, HBM, HBM, HBM]
    out_specs = [HBM] * 2
    out_shape = [pltpu.HBM((count * QB, DV), F32), pltpu.HBM((count * QB, LANES), F32)]
    scratch = [
        pltpu.VMEM((count * QB, DV), F32),
        pltpu.VMEM((count * QB, LANES), F32),
        pltpu.VMEM((3 * BLOCKS, QB), F32),
        pltpu.VMEM((TOKS, DQK), BF16),
        pltpu.VMEM((TOKS, DQK), BF16),
        pltpu.VMEM((TOKS, DV), BF16),
        pltpu.SemaphoreType.DMA((3, BLOCKS)),
        pltpu.SemaphoreType.DMA((2, count)),
        pltpu.SemaphoreType.DMA(()),
    ]
    kernel = next_kernel
    if table is None:
        kernel = first_kernel
        out_specs += [HBM]
        out_shape += [pltpu.HBM((3 * BLOCKS, QB), F32)]
    if everything is not None:
        kernel = last_kernel
        args += [in_hbm(everything)]
        in_specs += [HBM]
        out_specs += [VMEM]
        out_shape += [pltpu.VMEM(everything.shape, F32)]
        scratch += [pltpu.SemaphoreType.DMA(())]
    return pl.pallas_call(
        functools.partial(kernel, blocks),
        in_specs=in_specs,
        out_specs=out_specs,
        out_shape=out_shape,
        scratch_shapes=scratch,
        compiler_params=pltpu.CompilerParams(vmem_limit_bytes=20 * MIB),
        cost_estimate=pl.CostEstimate(flops=800_000_000 * units, bytes_accessed=MIB * units, transcendentals=0),
        name="within_shard",
    )(*args)


def scale_kernel(mine_ref, table_hbm, q_hbm, *refs):
    count = len(PARTS)
    hbms, (pre_ref, carried_ref, q_ref, table_ref, den_ref, num_ref, table_sem, q_sem, sem) = refs[: 2 * count], refs[2 * count :]
    place = {i: (n, m) for n, blocks in enumerate(PARTS) for m, i in enumerate(blocks)}
    table_copy = pltpu.make_async_copy(table_hbm, table_ref, table_sem)
    table_copy.start()
    copies = []
    for i in range(BLOCKS):
        n, m = place[i]
        here, there = pl.ds(i * QB, QB), pl.ds(m * QB, QB)
        copies.append(
            (
                pltpu.make_async_copy(q_hbm.at[here], q_ref.at[here], q_sem.at[i]),
                pltpu.make_async_copy(hbms[2 * n + 1].at[there], den_ref.at[here], sem.at[1, i]),
                pltpu.make_async_copy(hbms[2 * n].at[there], num_ref.at[here], sem.at[0, i]),
            )
        )
        for copy in copies[-1]:
            copy.start()
    table_copy.wait()
    log_in = mine_ref[2:3, :]
    norm = jnp.concatenate([mine_ref[0:1, :], mine_ref[1:2, :]], axis=1)
    for i in range(BLOCKS):
        here = pl.ds(i * QB, QB)
        top = column(table_ref[2 * BLOCKS + i : 2 * BLOCKS + i + 1, :])
        peak = jnp.maximum(top, log_in)
        kept, carried = jnp.exp(top - peak), jnp.exp(log_in - peak)
        copies[i][0].wait()
        from_norm = jnp.sum(q_ref[here, :].astype(F32) * norm, axis=1, keepdims=True)
        copies[i][1].wait()
        denom = jnp.sum(den_ref[here, :], axis=1, keepdims=True) * kept + carried * from_norm
        inverse = 1.0 / jnp.maximum(jnp.abs(denom), 1.0)
        carried_ref[here, :] = carried * inverse
        copies[i][2].wait()
        pre_ref[here, :] = wide(kept * inverse, DV) * num_ref[here, :]
        log_in = log_in + table_ref[BLOCKS + i : BLOCKS + i + 1, :][:, QB - 1 :]


def scaled(table, mine, queries, pieces):
    refs = [in_hbm(a) for piece in pieces for a in piece]
    return pl.pallas_call(
        scale_kernel,
        in_specs=[VMEM] + [HBM] * (2 + len(refs)),
        out_specs=[VMEM] * 3,
        out_shape=[
            pltpu.VMEM((TOKS, DV), F32),
            pltpu.VMEM((TOKS, LANES), F32),
            pltpu.VMEM((TOKS, DQK), BF16),
        ],
        scratch_shapes=[
            pltpu.VMEM((3 * BLOCKS, QB), F32),
            pltpu.VMEM((TOKS, LANES), F32),
            pltpu.VMEM((TOKS, DV), F32),
            pltpu.SemaphoreType.DMA(()),
            pltpu.SemaphoreType.DMA((BLOCKS,)),
            pltpu.SemaphoreType.DMA((2, BLOCKS)),
        ],
        compiler_params=pltpu.CompilerParams(vmem_limit_bytes=12 * MIB),
        cost_estimate=pl.CostEstimate(flops=1_600_000_000, bytes_accessed=8 * MIB, transcendentals=0),
        name="row_scales",
    )(mine, in_hbm(table), in_hbm(queries), *refs)


def joined_kernel(x_ref, q_ref, own_ref, one_ref, two_ref, three_ref, carried_ref, pre_ref, out_hbm, mem_ref, mem_b_ref, out_ref, sem):
    x = x_ref[0]
    for k, ref in enumerate((own_ref, one_ref, two_ref, three_ref)):
        at = lax.rem(x + XS - k, XS)
        mem_ref[:, pl.ds(at, 1)] = ref[...].reshape(ZS, 1, ROWS, DV)
    mem_b_ref[...] = mem_ref[...].reshape(DQK, DV).astype(BF16)
    copies = []
    for i in range(BLOCKS):
        span = pl.ds(i * QB, QB)
        product = jnp.dot(q_ref[span, :], mem_b_ref[...], preferred_element_type=F32)
        out_ref[span, :] = (pre_ref[span, :] + wide(carried_ref[span, :], DV) * product).astype(BF16)
        copies.append(pltpu.make_async_copy(out_ref.at[span], out_hbm.at[span], sem.at[i]))
        copies[-1].start()
    for copy in copies:
        copy.wait()


def joined(x, queries, parts, carried, pre):
    return pl.pallas_call(
        joined_kernel,
        in_specs=[SMEM] + [VMEM] * 7,
        out_specs=HBM,
        out_shape=jax.ShapeDtypeStruct((TOKS, DV), BF16),
        scratch_shapes=[
            pltpu.VMEM((ZS, XS, ROWS, DV), F32),
            pltpu.VMEM((DQK, DV), BF16),
            pltpu.VMEM((TOKS, DV), BF16),
            pltpu.SemaphoreType.DMA((BLOCKS,)),
        ],
        compiler_params=pltpu.CompilerParams(vmem_limit_bytes=8 * MIB),
        cost_estimate=pl.CostEstimate(flops=600_000_000, bytes_accessed=9 * MIB, transcendentals=0),
        name="join_memory",
    )(x, queries, *parts, carried, pre)


def exchanged(x, axis):
    return lax.all_to_all(x, axis, split_axis=0, concat_axis=0, tiled=True)


def around(parts):
    moved = [parts[0]]
    for k in range(1, XS):
        moved.append(lax.ppermute(parts[k], "ctx_1", [(i, (i + k) % XS) for i in range(XS)]))
    return moved


def on_device(queries, keys, values, gate_pre):
    x = lax.axis_index("ctx_1").astype(jnp.int32).reshape(1)
    z = lax.axis_index("ctx_0").astype(jnp.int32).reshape(1)
    gates = exchanged(gate_sums(gate_pre), "head")
    keys_t = turned(keys)
    *parts, tick = state(x, gates, keys_t, values)
    moved = around(parts)
    qkv = (queries, keys, values)
    num_a, den_a, table = local(PARTS[0], gates, tick, *qkv)
    total, everything, small = grouped(x, moved, den_a)
    got = exchanged(total, "ctx_0")
    num_b, den_b = local(PARTS[1], None, small, *qkv, table)
    before, closing, final_norm, top, group, mine = chained(x, z, got, small, den_b)
    back = exchanged(before, "ctx_0")
    num_c, den_c, everything = local(PARTS[2], None, mine, *qkv, table, everything)
    *parts, mine = spread(x, back, everything, small, group, mine)
    moved = around(parts)
    pre, carried, q = scaled(table, mine, queries, [(num_a, den_a), (num_b, den_b), (num_c, den_c)])
    hidden = joined(x, q, moved, carried, pre)
    return (hidden, closing, final_norm, top[0, :1])


def solution(mesh):
    split = Mesh(mesh.devices.reshape(8, 4, mesh.shape["head"]), ("ctx_0", "ctx_1", "head"))
    in_specs = (P(CTX, "head"), P(CTX, "head"), P(CTX, "head"), P(None, None, CTX_HEAD))
    out_specs = (P(CTX, "head"), P("head", CTX, None), P("head", None), P("head"))
    return jax.shard_map(
        on_device, mesh=split, in_specs=in_specs, out_specs=out_specs, check_vma=False
    )
```

```python
import functools

import jax
import jax.numpy as jnp
from jax import lax
from jax.experimental import pallas as pl
from jax.experimental.pallas import tpu as pltpu
from jax.sharding import Mesh
from jax.sharding import PartitionSpec as P

DQK = 256
DV = 512
XS = 4
ZS = 8
ROWS = DQK // (XS * ZS)
SLICE = ZS * ROWS
SENT = SLICE + 8
PIECES = 8
PIECE = 256
LANES = 128
WIDE = DV + LANES
TOKS = PIECES * PIECE
QB = 512
BLOCKS = TOKS // QB
PARTS = ((3,), (0, 1), (2,))
CTX = ("ctx_0", "ctx_1")
CTX_HEAD = ("ctx_0", "ctx_1", "head")
NEG = -1e30
F32 = jnp.float32
BF16 = jnp.bfloat16
VMEM = pl.BlockSpec(memory_space=pltpu.VMEM)
HBM = pl.BlockSpec(memory_space=pltpu.HBM)
ANY = pl.BlockSpec(memory_space=pl.ANY)
MIB = 1 << 20


def place_of(axis):
    return lax.axis_index(axis).astype(jnp.int32)


def log_sigmoid(x):
    z = jnp.exp(-jnp.abs(x))
    s = z / (2.0 + z)
    s2 = s * s
    tail = jnp.full_like(s, 1.0 / 17.0)
    for n in (15, 13, 11, 9, 7, 5, 3, 1):
        tail = tail * s2 + 1.0 / n
    return jnp.minimum(x, 0.0) - 2.0 * s * tail


def three_parts(x):
    high = x.astype(BF16)
    rest = x - high.astype(F32)
    mid = rest.astype(BF16)
    low = (rest - mid.astype(F32)).astype(BF16)
    return high, mid, low


def piece_sums(forget):
    n = forget.shape[1]
    upto = lax.broadcasted_iota(jnp.int32, (n, n), 0) <= lax.broadcasted_iota(jnp.int32, (n, n), 1)
    ones = jnp.where(upto, 1.0, 0.0).astype(BF16)
    parts = jnp.concatenate([p.astype(F32) for p in three_parts(log_sigmoid(forget))], axis=0)
    sums = jnp.dot(parts.astype(BF16), ones, preferred_element_type=F32)
    k = forget.shape[0]
    return sums[:k] + sums[k : 2 * k] + sums[2 * k :]


def gate_kernel(g_ref, out_ref):
    cum = piece_sums(g_ref[1])
    own = g_ref[0] - cum
    for h in range(own.shape[0]):
        out_ref[h, 0:1, :] = own[h : h + 1]
        out_ref[h, 1:2, :] = cum[h : h + 1]


def gate_sums(gate_pre):
    kinds, heads, n = gate_pre.shape
    return pl.pallas_call(
        gate_kernel,
        in_specs=[VMEM],
        out_specs=VMEM,
        out_shape=pltpu.VMEM((heads, kinds, n), F32),
        compiler_params=pltpu.CompilerParams(vmem_limit_bytes=8 * MIB),
        name="gate_sums",
    )(gate_pre)


def turned_kernel(k_ref, kt_ref):
    kt_ref[...] = k_ref[...].T


def turned(keys):
    return pl.pallas_call(
        turned_kernel,
        grid=(4,),
        in_specs=[pl.BlockSpec((TOKS // 4, DQK), lambda i: (i, 0))],
        out_specs=pl.BlockSpec((DQK, TOKS // 4), lambda i: (0, i)),
        out_shape=jax.ShapeDtypeStruct((DQK, TOKS), BF16),
        compiler_params=pltpu.CompilerParams(vmem_limit_bytes=8 * MIB),
        cost_estimate=pl.CostEstimate(flops=0, bytes_accessed=4 * MIB, transcendentals=0),
        name="turn_keys",
    )(keys)


def state_kernel(g_ref, kt_ref, v_ref, own_ref, one_ref, two_ref, three_ref, tick_ref, w_ref, acc_ref):
    own = g_ref[:, 0, :]
    cum = g_ref[:, 1, :]
    later = jnp.broadcast_to(cum[:, PIECE - 1 :], cum.shape)
    row = lax.broadcasted_iota(jnp.int32, cum.shape, 0)
    for shift in (1, 2, 4):
        moved = pltpu.roll(later, PIECES - shift, 0)
        later = later + jnp.where(row + shift < PIECES, moved, 0.0)
    reach = own + later
    stab = jnp.max(jnp.max(reach, axis=1, keepdims=True), axis=0, keepdims=True)
    w_ref[...] = jnp.exp(reach - stab) * (DQK**-0.5)
    norm = jnp.zeros((24, DQK), F32)
    for j in range(BLOCKS):
        span = pl.ds(j * QB, QB)
        weight = jnp.concatenate([w_ref[2 * j : 2 * j + 1, :], w_ref[2 * j + 1 : 2 * j + 2, :]], axis=1)
        k = kt_ref[:, span]
        scaled = (k.astype(F32) * weight).astype(BF16)
        parts = [jnp.broadcast_to(p.astype(F32), (8, QB)) for p in three_parts(weight)]
        parts = jnp.concatenate(parts, axis=0).astype(BF16)
        norm += lax.dot_general(parts, k, (((1,), (1,)), ((), ())), preferred_element_type=F32)
        product = jnp.dot(scaled, v_ref[span, :], preferred_element_type=F32)
        if j:
            product += acc_ref[...].reshape(DQK, DV)
        acc_ref[...] = product.reshape(ZS, XS, ROWS, DV)
    norm = norm[0:8] + norm[8:16] + norm[16:24]
    norm = jnp.concatenate([norm, norm], axis=1)
    extra = tail_of(norm[0:1], stab, later[0:1, 0:1])
    x = place_of("ctx_1")
    for k, ref in enumerate((own_ref, one_ref, two_ref, three_ref)):
        to = lax.rem(x + k, XS)
        ref[0:SLICE, :] = acc_ref[:, pl.ds(to, 1)].reshape(SLICE, DV)
        ref[SLICE:, :] = extra
    tick_ref[...] = extra[:, :LANES]


def state(gates, keys_t, values):
    return pl.pallas_call(
        state_kernel,
        in_specs=[VMEM, VMEM, VMEM],
        out_specs=[VMEM] * 5,
        out_shape=[jax.ShapeDtypeStruct((SENT, DV), F32)] * 4 + [jax.ShapeDtypeStruct((8, LANES), F32)],
        scratch_shapes=[
            pltpu.VMEM((PIECES, PIECE), F32),
            pltpu.VMEM((ZS, XS, ROWS, DV), F32),
        ],
        compiler_params=pltpu.CompilerParams(vmem_limit_bytes=12 * MIB),
        cost_estimate=pl.CostEstimate(flops=600_000_000, bytes_accessed=5 * MIB, transcendentals=0),
        name="shard_state",
    )(gates, keys_t, values)


def tail_of(norm, stab, total):
    row = lax.broadcasted_iota(jnp.int32, (8, DV), 0)
    return jnp.where(row == 0, norm, jnp.where(row == 1, stab, total))


def pieces_of(tail):
    return tail[0:1, :], tail[1:2, :], tail[2:3, :]


def chain_of(early, late):
    norm_e, stab_e, total_e = early
    norm_l, stab_l, total_l = late
    shifted = stab_e + total_l
    stab = jnp.maximum(shifted, stab_l)
    keep, take = jnp.exp(shifted - stab), jnp.exp(stab_l - stab)
    return keep, take, (keep * norm_e + take * norm_l, stab, total_e + total_l)


def group_kernel(own_ref, one_ref, two_ref, three_ref, after_ref, out_ref, all_ref):
    x = place_of("ctx_1")
    for k, ref in enumerate((own_ref, one_ref, two_ref, three_ref)):
        at = lax.rem(x + XS - k, XS)
        all_ref[pl.ds(at, 1)] = ref[...].reshape(1, SENT, DV)
    small = pieces_of(all_ref[0, SLICE:, :])
    factors = []
    for j in range(1, XS):
        keep, take, small = chain_of(small, pieces_of(all_ref[j, SLICE:, :]))
        factors.append((keep, take))
    for at in range(0, SLICE, ROWS):
        memory = all_ref[0, at : at + ROWS, :]
        for j, (keep, take) in enumerate(factors):
            memory = keep * memory + take * all_ref[j + 1, at : at + ROWS, :]
        out_ref[at : at + ROWS, :] = memory
    out_ref[SLICE:, :] = tail_of(*small)


def grouped(parts, after):
    return pl.pallas_call(
        group_kernel,
        in_specs=[VMEM] * 4 + [ANY],
        out_specs=[VMEM] * 2,
        out_shape=[
            jax.ShapeDtypeStruct((SENT, DV), F32),
            jax.ShapeDtypeStruct((XS, SENT, DV), F32),
        ],
        compiler_params=pltpu.CompilerParams(vmem_limit_bytes=4 * MIB),
        cost_estimate=pl.CostEstimate(flops=1_000_000, bytes_accessed=2 * MIB, transcendentals=0),
        name="group_states",
    )(*parts, after)


def merge(later, total_ref, got_ref, prefix_ref, new_total, new_prefix):
    own, got = pieces_of(total_ref[SLICE:, :]), pieces_of(got_ref[SLICE:, :])
    first = [jnp.where(later, g, o) for g, o in zip(got, own)]
    second = [jnp.where(later, o, g) for g, o in zip(got, own)]
    keep, take, small = chain_of(first, second)
    f_own, f_got = jnp.where(later, take, keep), jnp.where(later, keep, take)
    for at in range(0, SLICE, ROWS):
        here = slice(at, at + ROWS)
        new_total[here, :] = f_own * total_ref[here, :] + f_got * got_ref[here, :]
    new_total[SLICE:, :] = tail_of(*small)
    if prefix_ref is None:
        before = (jnp.zeros((1, DV), F32), jnp.full((1, DV), NEG, F32), jnp.zeros((1, DV), F32))
    else:
        before = pieces_of(prefix_ref[SLICE:, :])
    bring, hold, small = chain_of(got, before)
    bring, hold = jnp.where(later, bring, 0.0), jnp.where(later, hold, 1.0)
    for at in range(0, SLICE, ROWS):
        here = slice(at, at + ROWS)
        memory = bring * got_ref[here, :]
        if prefix_ref is not None:
            memory = memory + hold * prefix_ref[here, :]
        new_prefix[here, :] = memory
    new_prefix[SLICE:, :] = tail_of(*[jnp.where(later, n, o) for n, o in zip(small, before)])


def later_of(z, bit):
    return lax.rem(lax.div(z, 1 << bit), 2) == 1


def first_round_kernel(total_ref, got_ref, after_ref, new_total, new_prefix):
    merge(later_of(place_of("ctx_0"), 0), total_ref, got_ref, None, new_total, new_prefix)


def next_round_kernel(total_ref, got_ref, prefix_ref, after_ref, new_total, new_prefix):
    merge(later_of(place_of("ctx_0"), 1), total_ref, got_ref, prefix_ref, new_total, new_prefix)


def round_of(kernel, *args):
    return pl.pallas_call(
        kernel,
        in_specs=[VMEM] * (len(args) - 1) + [ANY],
        out_specs=[VMEM] * 2,
        out_shape=[jax.ShapeDtypeStruct((SENT, DV), F32)] * 2,
        compiler_params=pltpu.CompilerParams(vmem_limit_bytes=4 * MIB),
        cost_estimate=pl.CostEstimate(flops=1_000_000, bytes_accessed=MIB, transcendentals=0),
        name="merge_round",
    )(*args)


def spread_kernel(total_ref, got_ref, prefix_ref, all_ref, after_ref, own_ref, one_ref, two_ref, three_ref, mine_ref, close_ref, norm_ref, top_ref, sum_ref, before_ref, out_ref):
    x, z = place_of("ctx_1"), place_of("ctx_0")
    merge(later_of(z, 2), total_ref, got_ref, prefix_ref, sum_ref, before_ref)
    close_ref[0] = sum_ref[pl.ds(pl.multiple_of(z * ROWS, ROWS), ROWS), :]
    norm, top, _ = pieces_of(sum_ref[SLICE:, :])
    norm_ref[...] = norm[:, :DQK]
    top_ref[...] = top[:, :LANES]
    small = pieces_of(before_ref[SLICE:, :])
    mine = small
    factors = []
    for j in range(XS - 1):
        keep, take, small = chain_of(small, pieces_of(all_ref[j, SLICE:, :]))
        mine = [jnp.where(x == j + 1, n, o) for n, o in zip(small, mine)]
        factors.append((keep, take))
    for at in range(0, SLICE, ROWS):
        memory = before_ref[at : at + ROWS, :]
        out_ref[0, at : at + ROWS, :] = memory
        for j, (keep, take) in enumerate(factors):
            memory = keep * memory + take * all_ref[j, at : at + ROWS, :]
            out_ref[j + 1, at : at + ROWS, :] = memory
    for k, ref in enumerate((own_ref, one_ref, two_ref, three_ref)):
        ref[...] = out_ref[pl.ds(lax.rem(x + k, XS), 1)].reshape(ZS, ROWS, DV)
    mine_ref[...] = tail_of(*mine)


def spread(total, got, prefix, everything, after):
    return pl.pallas_call(
        spread_kernel,
        in_specs=[VMEM] * 4 + [ANY],
        out_specs=[VMEM] * 8,
        out_shape=[jax.ShapeDtypeStruct((ZS, ROWS, DV), F32)] * 4
        + [
            jax.ShapeDtypeStruct((8, DV), F32),
            jax.ShapeDtypeStruct((1, ROWS, DV), F32),
            jax.ShapeDtypeStruct((1, DQK), F32),
            jax.ShapeDtypeStruct((1, LANES), F32),
        ],
        scratch_shapes=[
            pltpu.VMEM((SENT, DV), F32),
            pltpu.VMEM((SENT, DV), F32),
            pltpu.VMEM((XS, SLICE, DV), F32),
        ],
        compiler_params=pltpu.CompilerParams(vmem_limit_bytes=4 * MIB),
        cost_estimate=pl.CostEstimate(flops=1_000_000, bytes_accessed=2 * MIB, transcendentals=0),
        name="spread_prefixes",
    )(total, got, prefix, everything, after)


def wide(x, n):
    return jnp.concatenate([x] * (n // LANES), axis=1)


def column(row):
    n = row.shape[1]
    return jnp.concatenate(
        [
            jnp.broadcast_to(row[:, at : at + LANES], (LANES, LANES)).T
            for at in range(0, n, LANES)
        ],
        axis=0,
    )


def tables(g_ref, table_ref):
    own, cum = [], []
    for r in range(0, PIECES, 2):
        first = g_ref[r, 1:2, :][:, PIECE - 1 :]
        own.append(jnp.concatenate([g_ref[r, 0:1, :], g_ref[r + 1, 0:1, :] - first], axis=1))
        cum.append(jnp.concatenate([g_ref[r, 1:2, :], g_ref[r + 1, 1:2, :] + first], axis=1))
    own = jnp.concatenate(own, axis=0)
    cum = jnp.concatenate(cum, axis=0)
    table_ref[0:BLOCKS, :] = own
    table_ref[BLOCKS : 2 * BLOCKS, :] = cum
    lane = lax.broadcasted_iota(jnp.int32, (BLOCKS, QB), 1)
    top = own
    shift = 1
    while shift < QB:
        moved = pltpu.roll(top, shift, 1)
        top = jnp.maximum(top, jnp.where(lane >= shift, moved, NEG))
        shift *= 2
    stab = jnp.full((1, 1), NEG, F32)
    for r in range(BLOCKS):
        at = 2 * BLOCKS + r
        table_ref[at : at + 1, :] = jnp.maximum(top[r : r + 1], stab)
        stab = jnp.maximum(stab, top[r : r + 1, QB - 1 :]) + cum[r : r + 1, QB - 1 :]


def local_kernel(blocks, table_ref, tick_ref, q_ref, k_ref, v_ref, num_ref, den_ref):
    for n, i in enumerate(blocks):
        here = pl.ds(n * QB, QB)
        top = column(table_ref[2 * BLOCKS + i : 2 * BLOCKS + i + 1, :])
        q = q_ref[pl.ds(i * QB, QB), :]

        def scores(j):
            at = pl.ds(pl.multiple_of(j * QB, QB), QB)
            return lax.dot_general(q, k_ref[at, :], (((1,), (1,)), ((), ())), preferred_element_type=F32)

        def sums(j, mixed):
            at = pl.ds(pl.multiple_of(j * QB, QB), QB)
            lanes = sum(mixed[:, c : c + LANES] for c in range(0, QB, LANES))
            return lanes, jnp.dot(mixed.astype(BF16), v_ref[at, :], preferred_element_type=F32)

        past = lax.broadcasted_iota(jnp.int32, (QB, QB), 0) >= lax.broadcasted_iota(jnp.int32, (QB, QB), 1)
        power = jnp.where(past, table_ref[i : i + 1, :] - wide(top, QB), NEG)
        den_ref[here, :], num_ref[here, :] = sums(i, jnp.exp(power) * scores(i))

        def earlier(m, shift):
            j = i - 1 - m
            shift = shift + table_ref[pl.ds(BLOCKS + j, 1), :][:, QB - 1 :]
            reach = table_ref[pl.ds(j, 1), :]
            peak = jnp.max(reach, axis=1, keepdims=True)
            lanes, product = sums(j, scores(j) * jnp.exp(reach - peak))
            factor = jnp.exp((peak + shift) - top)
            den_ref[here, :] += factor * lanes
            num_ref[here, :] += wide(factor, DV) * product
            return shift

        if i:
            lax.fori_loop(0, i, earlier, jnp.zeros((1, 1), F32))


def first_kernel(blocks, g_ref, tick_ref, q_ref, k_ref, v_ref, num_ref, den_ref, table_ref):
    tables(g_ref, table_ref)
    local_kernel(blocks, table_ref, tick_ref, q_ref, k_ref, v_ref, num_ref, den_ref)


def local(blocks, gates, tick, queries, keys, values, table=None):
    count = len(blocks)
    units = sum(blocks) + count
    first = table is None
    out_shape = [
        jax.ShapeDtypeStruct((count * QB, DV), F32),
        jax.ShapeDtypeStruct((count * QB, LANES), F32),
        jax.ShapeDtypeStruct((3 * BLOCKS, QB), F32),
    ][: 3 if first else 2]
    return pl.pallas_call(
        functools.partial(first_kernel if first else local_kernel, blocks),
        in_specs=[VMEM, ANY] + [VMEM] * 3,
        out_specs=[VMEM] * len(out_shape),
        out_shape=out_shape,
        compiler_params=pltpu.CompilerParams(vmem_limit_bytes=8 * MIB),
        cost_estimate=pl.CostEstimate(flops=800_000_000 * units, bytes_accessed=MIB * units, transcendentals=0),
        name="within_shard",
    )(gates if first else table, tick, queries, keys, values)


def scale_kernel(table_ref, mine_ref, q_ref, *refs):
    dens, (kept_ref, carried_ref) = refs[:-2], refs[-2:]
    norm, log_in, _ = pieces_of(mine_ref)
    norm, log_in = norm[:, :DQK], log_in[:, :LANES]
    place = {i: (dens[n], m) for n, blocks in enumerate(PARTS) for m, i in enumerate(blocks)}
    for i in range(BLOCKS):
        den_ref, m = place[i]
        here, there = pl.ds(i * QB, QB), pl.ds(m * QB, QB)
        top = column(table_ref[2 * BLOCKS + i : 2 * BLOCKS + i + 1, :])
        peak = jnp.maximum(top, log_in)
        kept, carried = jnp.exp(top - peak) * (DQK**-0.5), jnp.exp(log_in - peak)
        from_norm = jnp.sum(q_ref[here, :].astype(F32) * norm, axis=1, keepdims=True)
        denom = jnp.sum(den_ref[there, :], axis=1, keepdims=True) * kept + carried * from_norm
        inverse = 1.0 / jnp.maximum(jnp.abs(denom), 1.0)
        kept_ref[here, :] = kept * inverse
        carried_ref[here, :] = carried * inverse
        log_in = log_in + table_ref[BLOCKS + i : BLOCKS + i + 1, :][:, QB - 1 :]


def scales(table, mine, queries, dens):
    return pl.pallas_call(
        scale_kernel,
        in_specs=[VMEM] * (3 + len(dens)),
        out_specs=[VMEM] * 2,
        out_shape=[jax.ShapeDtypeStruct((TOKS, LANES), F32)] * 2,
        compiler_params=pltpu.CompilerParams(vmem_limit_bytes=4 * MIB),
        cost_estimate=pl.CostEstimate(flops=600_000_000, bytes_accessed=4 * MIB, transcendentals=0),
        name="row_scales",
    )(table, mine, queries, *dens)


def joined_kernel(q_ref, own_ref, one_ref, two_ref, three_ref, kept_ref, carried_ref, *refs):
    nums, (out_hbm, mem_ref, mem_b_ref, out_ref, sem) = refs[:-5], refs[-5:]
    x = place_of("ctx_1")
    for k, ref in enumerate((own_ref, one_ref, two_ref, three_ref)):
        at = lax.rem(x + XS - k, XS)
        mem_ref[:, pl.ds(at, 1)] = ref[...].reshape(ZS, 1, ROWS, DV)
    mem_b_ref[...] = mem_ref[...].reshape(DQK, DV).astype(BF16)
    copies = []
    for n, blocks in enumerate(PARTS):
        for m, i in enumerate(blocks):
            for half in range(0, QB, PIECE):
                span, there = pl.ds(i * QB + half, PIECE), pl.ds(m * QB + half, PIECE)
                product = jnp.dot(q_ref[span, :], mem_b_ref[...], preferred_element_type=F32)
                local_part = wide(kept_ref[span, :], DV) * nums[n][there, :]
                out_ref[span, :] = (local_part + wide(carried_ref[span, :], DV) * product).astype(BF16)
                copies.append(pltpu.make_async_copy(out_ref.at[span], out_hbm.at[span], sem.at[len(copies)]))
                copies[-1].start()
    for copy in copies:
        copy.wait()


def joined(queries, parts, kept, carried, nums):
    return pl.pallas_call(
        joined_kernel,
        in_specs=[VMEM] * (7 + len(nums)),
        out_specs=HBM,
        out_shape=jax.ShapeDtypeStruct((TOKS, DV), BF16),
        scratch_shapes=[
            pltpu.VMEM((ZS, XS, ROWS, DV), F32),
            pltpu.VMEM((DQK, DV), BF16),
            pltpu.VMEM((TOKS, DV), BF16),
            pltpu.SemaphoreType.DMA((PIECES,)),
        ],
        compiler_params=pltpu.CompilerParams(vmem_limit_bytes=8 * MIB),
        cost_estimate=pl.CostEstimate(flops=600_000_000, bytes_accessed=9 * MIB, transcendentals=0),
        name="join_memory",
    )(queries, *parts, kept, carried, *nums)


def exchanged(x, axis):
    return lax.all_to_all(x, axis, split_axis=0, concat_axis=0, tiled=True)


def around(parts):
    moved = [parts[0]]
    for k in range(1, XS):
        moved.append(lax.ppermute(parts[k], "ctx_1", [(i, (i + k) % XS) for i in range(XS)]))
    return moved


def swapped(x, partner):
    return lax.ppermute(x, "ctx_0", [(i, partner(i)) for i in range(ZS)])


def on_device(queries, keys, values, gate_pre):
    gates = exchanged(gate_sums(gate_pre), "head")
    keys_t = turned(keys)
    *parts, tick = state(gates, keys_t, values)
    moved = around(parts)
    qkv = (queries, keys, values)
    num_a, den_a, table = local(PARTS[0], gates, tick, *qkv)
    total, everything = grouped(moved, den_a)
    got = swapped(total, lambda i: i ^ 1)
    total, prefix = round_of(first_round_kernel, total, got, den_a)
    got = swapped(total, lambda i: i ^ 2)
    num_b, den_b = local(PARTS[1], None, prefix, *qkv, table)
    total, prefix = round_of(next_round_kernel, total, got, prefix, den_b)
    got = swapped(total, lambda i: ZS - 1 - i)
    num_c, den_c = local(PARTS[2], None, prefix, *qkv, table)
    *parts, mine, closing, final_norm, top = spread(total, got, prefix, everything, den_c)
    moved = around(parts)
    kept, carried = scales(table, mine, queries, [den_a, den_b, den_c])
    hidden = joined(queries, moved, kept, carried, [num_a, num_b, num_c])
    return (hidden, closing, final_norm, top[0, :1])


def solution(mesh):
    split = Mesh(mesh.devices.reshape(8, 4, mesh.shape["head"]), ("ctx_0", "ctx_1", "head"))
    in_specs = (P(CTX, "head"), P(CTX, "head"), P(CTX, "head"), P(None, None, CTX_HEAD))
    out_specs = (P(CTX, "head"), P("head", CTX, None), P("head", None), P("head"))
    return jax.shard_map(
        on_device, mesh=split, in_specs=in_specs, out_specs=out_specs, check_vma=False
    )
```

```python
import functools

import jax
import jax.numpy as jnp
from jax import lax
from jax.experimental import pallas as pl
from jax.experimental.pallas import tpu as pltpu
from jax.sharding import Mesh
from jax.sharding import PartitionSpec as P

DQK = 256
DV = 512
XS = 4
ZS = 8
ROWS = DQK // (XS * ZS)
SLICE = ZS * ROWS
SENT = SLICE + 8
PIECES = 8
PIECE = 256
LANES = 128
WIDE = DV + LANES
TOKS = PIECES * PIECE
QB = 512
BLOCKS = TOKS // QB
PARTS = ((3,), (0, 1), (2,))
CTX = ("ctx_0", "ctx_1")
CTX_HEAD = ("ctx_0", "ctx_1", "head")
NEG = -1e30
F32 = jnp.float32
BF16 = jnp.bfloat16
VMEM = pl.BlockSpec(memory_space=pltpu.VMEM)
HBM = pl.BlockSpec(memory_space=pltpu.HBM)
ANY = pl.BlockSpec(memory_space=pl.ANY)
MIB = 1 << 20


def in_hbm(x):
    return pltpu.with_memory_space_constraint(x, pltpu.HBM)


def place_of(axis):
    return lax.axis_index(axis).astype(jnp.int32)


def log_sigmoid(x):
    z = jnp.exp(-jnp.abs(x))
    s = z / (2.0 + z)
    s2 = s * s
    tail = jnp.full_like(s, 1.0 / 17.0)
    for n in (15, 13, 11, 9, 7, 5, 3, 1):
        tail = tail * s2 + 1.0 / n
    return jnp.minimum(x, 0.0) - 2.0 * s * tail


def three_parts(x):
    high = x.astype(BF16)
    rest = x - high.astype(F32)
    mid = rest.astype(BF16)
    low = (rest - mid.astype(F32)).astype(BF16)
    return high, mid, low


def piece_sums(forget):
    n = forget.shape[1]
    upto = lax.broadcasted_iota(jnp.int32, (n, n), 0) <= lax.broadcasted_iota(jnp.int32, (n, n), 1)
    ones = jnp.where(upto, 1.0, 0.0).astype(BF16)
    parts = jnp.concatenate([p.astype(F32) for p in three_parts(log_sigmoid(forget))], axis=0)
    sums = jnp.dot(parts.astype(BF16), ones, preferred_element_type=F32)
    k = forget.shape[0]
    return sums[:k] + sums[k : 2 * k] + sums[2 * k :]


def gate_kernel(g_hbm, out_ref, g_ref, sem):
    copy = pltpu.make_async_copy(g_hbm, g_ref, sem)
    copy.start()
    copy.wait()
    cum = piece_sums(g_ref[1])
    own = g_ref[0] - cum
    for h in range(own.shape[0]):
        out_ref[h, 0:1, :] = own[h : h + 1]
        out_ref[h, 1:2, :] = cum[h : h + 1]


def gate_sums(gate_pre):
    kinds, heads, n = gate_pre.shape
    return pl.pallas_call(
        gate_kernel,
        in_specs=[HBM],
        out_specs=VMEM,
        out_shape=jax.ShapeDtypeStruct((heads, kinds, n), F32),
        scratch_shapes=[pltpu.VMEM(gate_pre.shape, F32), pltpu.SemaphoreType.DMA(())],
        compiler_params=pltpu.CompilerParams(vmem_limit_bytes=4 * MIB),
        name="gate_sums",
    )(in_hbm(gate_pre))


def turned_kernel(k_hbm, v_hbm, kt_ref, v_ref, k_ref, k_sem, v_sem):
    copies = []
    for j in range(BLOCKS):
        span = pl.ds(j * QB, QB)
        copies.append(pltpu.make_async_copy(k_hbm.at[span], k_ref.at[span], k_sem.at[j]))
        copies[-1].start()
    values = pltpu.make_async_copy(v_hbm, v_ref, v_sem)
    values.start()
    for j in range(BLOCKS):
        span = pl.ds(j * QB, QB)
        copies[j].wait()
        kt_ref[:, span] = k_ref[span, :].T
    values.wait()


def turned(keys, values):
    return pl.pallas_call(
        turned_kernel,
        in_specs=[HBM] * 2,
        out_specs=[VMEM] * 2,
        out_shape=[jax.ShapeDtypeStruct((DQK, TOKS), BF16), jax.ShapeDtypeStruct((TOKS, DV), BF16)],
        scratch_shapes=[
            pltpu.VMEM((TOKS, DQK), BF16),
            pltpu.SemaphoreType.DMA((BLOCKS,)),
            pltpu.SemaphoreType.DMA(()),
        ],
        compiler_params=pltpu.CompilerParams(vmem_limit_bytes=4 * MIB),
        cost_estimate=pl.CostEstimate(flops=0, bytes_accessed=4 * MIB, transcendentals=0),
        name="turn_keys",
    )(in_hbm(keys), in_hbm(values))


def state_kernel(g_ref, kt_ref, v_ref, own_ref, one_ref, two_ref, three_ref, tick_ref, w_ref, acc_ref):
    own = g_ref[:, 0, :]
    cum = g_ref[:, 1, :]
    later = jnp.broadcast_to(cum[:, PIECE - 1 :], cum.shape)
    row = lax.broadcasted_iota(jnp.int32, cum.shape, 0)
    for shift in (1, 2, 4):
        moved = pltpu.roll(later, PIECES - shift, 0)
        later = later + jnp.where(row + shift < PIECES, moved, 0.0)
    reach = own + later
    stab = jnp.max(jnp.max(reach, axis=1, keepdims=True), axis=0, keepdims=True)
    w_ref[...] = jnp.exp(reach - stab) * (DQK**-0.5)
    norm = jnp.zeros((24, DQK), F32)
    for j in range(BLOCKS):
        span = pl.ds(j * QB, QB)
        weight = jnp.concatenate([w_ref[2 * j : 2 * j + 1, :], w_ref[2 * j + 1 : 2 * j + 2, :]], axis=1)
        k = kt_ref[:, span]
        scaled = (k.astype(F32) * weight).astype(BF16)
        parts = [jnp.broadcast_to(p.astype(F32), (8, QB)) for p in three_parts(weight)]
        parts = jnp.concatenate(parts, axis=0).astype(BF16)
        norm += lax.dot_general(parts, k, (((1,), (1,)), ((), ())), preferred_element_type=F32)
        product = jnp.dot(scaled, v_ref[span, :], preferred_element_type=F32)
        if j:
            product += acc_ref[...].reshape(DQK, DV)
        acc_ref[...] = product.reshape(ZS, XS, ROWS, DV)
    norm = norm[0:8] + norm[8:16] + norm[16:24]
    norm = jnp.concatenate([norm, norm], axis=1)
    extra = tail_of(norm[0:1], stab, later[0:1, 0:1])
    x = place_of("ctx_1")
    for k, ref in enumerate((own_ref, one_ref, two_ref, three_ref)):
        to = lax.rem(x + k, XS)
        ref[0:SLICE, :] = acc_ref[:, pl.ds(to, 1)].reshape(SLICE, DV)
        ref[SLICE:, :] = extra
    tick_ref[...] = extra[:, :LANES]


def state(gates, keys_t, values):
    return pl.pallas_call(
        state_kernel,
        in_specs=[VMEM, VMEM, VMEM],
        out_specs=[VMEM] * 5,
        out_shape=[jax.ShapeDtypeStruct((SENT, DV), F32)] * 4 + [jax.ShapeDtypeStruct((8, LANES), F32)],
        scratch_shapes=[
            pltpu.VMEM((PIECES, PIECE), F32),
            pltpu.VMEM((ZS, XS, ROWS, DV), F32),
        ],
        compiler_params=pltpu.CompilerParams(vmem_limit_bytes=12 * MIB),
        cost_estimate=pl.CostEstimate(flops=600_000_000, bytes_accessed=5 * MIB, transcendentals=0),
        name="shard_state",
    )(gates, keys_t, values)


def tail_of(norm, stab, total):
    row = lax.broadcasted_iota(jnp.int32, (8, DV), 0)
    return jnp.where(row == 0, norm, jnp.where(row == 1, stab, total))


def pieces_of(tail):
    return tail[0:1, :], tail[1:2, :], tail[2:3, :]


def chain_of(early, late):
    norm_e, stab_e, total_e = early
    norm_l, stab_l, total_l = late
    shifted = stab_e + total_l
    stab = jnp.maximum(shifted, stab_l)
    keep, take = jnp.exp(shifted - stab), jnp.exp(stab_l - stab)
    return keep, take, (keep * norm_e + take * norm_l, stab, total_e + total_l)


def group_kernel(own_ref, one_ref, two_ref, three_ref, after_ref, out_ref, all_ref):
    x = place_of("ctx_1")
    for k, ref in enumerate((own_ref, one_ref, two_ref, three_ref)):
        at = lax.rem(x + XS - k, XS)
        all_ref[pl.ds(at, 1)] = ref[...].reshape(1, SENT, DV)
    small = pieces_of(all_ref[0, SLICE:, :])
    factors = []
    for j in range(1, XS):
        keep, take, small = chain_of(small, pieces_of(all_ref[j, SLICE:, :]))
        factors.append((keep, take))
    for at in range(0, SLICE, ROWS):
        memory = all_ref[0, at : at + ROWS, :]
        for j, (keep, take) in enumerate(factors):
            memory = keep * memory + take * all_ref[j + 1, at : at + ROWS, :]
        out_ref[at : at + ROWS, :] = memory
    out_ref[SLICE:, :] = tail_of(*small)


def grouped(parts, after):
    return pl.pallas_call(
        group_kernel,
        in_specs=[VMEM] * 4 + [ANY],
        out_specs=[VMEM] * 2,
        out_shape=[
            jax.ShapeDtypeStruct((SENT, DV), F32),
            jax.ShapeDtypeStruct((XS, SENT, DV), F32),
        ],
        compiler_params=pltpu.CompilerParams(vmem_limit_bytes=4 * MIB),
        cost_estimate=pl.CostEstimate(flops=1_000_000, bytes_accessed=2 * MIB, transcendentals=0),
        name="group_states",
    )(*parts, after)


def merge(later, total_ref, got_ref, prefix_ref, new_total, new_prefix):
    own, got = pieces_of(total_ref[SLICE:, :]), pieces_of(got_ref[SLICE:, :])
    first = [jnp.where(later, g, o) for g, o in zip(got, own)]
    second = [jnp.where(later, o, g) for g, o in zip(got, own)]
    keep, take, small = chain_of(first, second)
    f_own, f_got = jnp.where(later, take, keep), jnp.where(later, keep, take)
    for at in range(0, SLICE, ROWS):
        here = slice(at, at + ROWS)
        new_total[here, :] = f_own * total_ref[here, :] + f_got * got_ref[here, :]
    new_total[SLICE:, :] = tail_of(*small)
    if prefix_ref is None:
        before = (jnp.zeros((1, DV), F32), jnp.full((1, DV), NEG, F32), jnp.zeros((1, DV), F32))
    else:
        before = pieces_of(prefix_ref[SLICE:, :])
    bring, hold, small = chain_of(got, before)
    bring, hold = jnp.where(later, bring, 0.0), jnp.where(later, hold, 1.0)
    for at in range(0, SLICE, ROWS):
        here = slice(at, at + ROWS)
        memory = bring * got_ref[here, :]
        if prefix_ref is not None:
            memory = memory + hold * prefix_ref[here, :]
        new_prefix[here, :] = memory
    new_prefix[SLICE:, :] = tail_of(*[jnp.where(later, n, o) for n, o in zip(small, before)])


def later_of(z, bit):
    return lax.rem(lax.div(z, 1 << bit), 2) == 1


def first_round_kernel(total_ref, got_ref, after_ref, new_total, new_prefix):
    merge(later_of(place_of("ctx_0"), 0), total_ref, got_ref, None, new_total, new_prefix)


def next_round_kernel(total_ref, got_ref, prefix_ref, after_ref, new_total, new_prefix):
    merge(later_of(place_of("ctx_0"), 1), total_ref, got_ref, prefix_ref, new_total, new_prefix)


def round_of(kernel, *args):
    return pl.pallas_call(
        kernel,
        in_specs=[VMEM] * (len(args) - 1) + [ANY],
        out_specs=[VMEM] * 2,
        out_shape=[jax.ShapeDtypeStruct((SENT, DV), F32)] * 2,
        compiler_params=pltpu.CompilerParams(vmem_limit_bytes=4 * MIB),
        cost_estimate=pl.CostEstimate(flops=1_000_000, bytes_accessed=MIB, transcendentals=0),
        name="merge_round",
    )(*args)


def spread_kernel(got_ref, prefix_ref, all_ref, after_ref, own_ref, one_ref, two_ref, three_ref, mine_ref, out_ref):
    x = place_of("ctx_1")
    later = later_of(place_of("ctx_0"), 2)
    before = pieces_of(prefix_ref[SLICE:, :])
    bring, hold, small = chain_of(pieces_of(got_ref[SLICE:, :]), before)
    bring, hold = jnp.where(later, bring, 0.0), jnp.where(later, hold, 1.0)
    small = [jnp.where(later, n, o) for n, o in zip(small, before)]
    mine = small
    factors = []
    for j in range(XS - 1):
        keep, take, small = chain_of(small, pieces_of(all_ref[j, SLICE:, :]))
        mine = [jnp.where(x == j + 1, n, o) for n, o in zip(small, mine)]
        factors.append((keep, take))
    for at in range(0, SLICE, ROWS):
        here = slice(at, at + ROWS)
        memory = bring * got_ref[here, :] + hold * prefix_ref[here, :]
        out_ref[0, here, :] = memory
        for j, (keep, take) in enumerate(factors):
            memory = keep * memory + take * all_ref[j, here, :]
            out_ref[j + 1, here, :] = memory
    for k, ref in enumerate((own_ref, one_ref, two_ref, three_ref)):
        ref[...] = out_ref[pl.ds(lax.rem(x + k, XS), 1)].reshape(ZS, ROWS, DV)
    mine_ref[...] = tail_of(*mine)


def spread(got, prefix, everything, after):
    return pl.pallas_call(
        spread_kernel,
        in_specs=[VMEM] * 3 + [ANY],
        out_specs=[VMEM] * 5,
        out_shape=[jax.ShapeDtypeStruct((ZS, ROWS, DV), F32)] * 4 + [jax.ShapeDtypeStruct((8, DV), F32)],
        scratch_shapes=[pltpu.VMEM((XS, SLICE, DV), F32)],
        compiler_params=pltpu.CompilerParams(vmem_limit_bytes=4 * MIB),
        cost_estimate=pl.CostEstimate(flops=1_000_000, bytes_accessed=2 * MIB, transcendentals=0),
        name="spread_prefixes",
    )(got, prefix, everything, after)


def wide(x, n):
    return jnp.concatenate([x] * (n // LANES), axis=1)


def column(row):
    n = row.shape[1]
    return jnp.concatenate(
        [
            jnp.broadcast_to(row[:, at : at + LANES], (LANES, LANES)).T
            for at in range(0, n, LANES)
        ],
        axis=0,
    )


def tables(g_ref, table_ref):
    own, cum = [], []
    for r in range(0, PIECES, 2):
        first = g_ref[r, 1:2, :][:, PIECE - 1 :]
        own.append(jnp.concatenate([g_ref[r, 0:1, :], g_ref[r + 1, 0:1, :] - first], axis=1))
        cum.append(jnp.concatenate([g_ref[r, 1:2, :], g_ref[r + 1, 1:2, :] + first], axis=1))
    own = jnp.concatenate(own, axis=0)
    cum = jnp.concatenate(cum, axis=0)
    table_ref[0:BLOCKS, :] = own
    table_ref[BLOCKS : 2 * BLOCKS, :] = cum
    lane = lax.broadcasted_iota(jnp.int32, (BLOCKS, QB), 1)
    top = own
    shift = 1
    while shift < QB:
        moved = pltpu.roll(top, shift, 1)
        top = jnp.maximum(top, jnp.where(lane >= shift, moved, NEG))
        shift *= 2
    stab = jnp.full((1, 1), NEG, F32)
    for r in range(BLOCKS):
        at = 2 * BLOCKS + r
        table_ref[at : at + 1, :] = jnp.maximum(top[r : r + 1], stab)
        stab = jnp.maximum(stab, top[r : r + 1, QB - 1 :]) + cum[r : r + 1, QB - 1 :]


def local_kernel(blocks, table_ref, tick_ref, q_ref, k_ref, v_ref, num_ref, den_ref):
    for n, i in enumerate(blocks):
        here = pl.ds(n * QB, QB)
        top = column(table_ref[2 * BLOCKS + i : 2 * BLOCKS + i + 1, :])
        q = q_ref[pl.ds(i * QB, QB), :]

        def scores(j):
            at = pl.ds(pl.multiple_of(j * QB, QB), QB)
            return lax.dot_general(q, k_ref[at, :], (((1,), (1,)), ((), ())), preferred_element_type=F32)

        def sums(j, mixed):
            at = pl.ds(pl.multiple_of(j * QB, QB), QB)
            lanes = sum(mixed[:, c : c + LANES] for c in range(0, QB, LANES))
            return lanes, jnp.dot(mixed.astype(BF16), v_ref[at, :], preferred_element_type=F32)

        past = lax.broadcasted_iota(jnp.int32, (QB, QB), 0) >= lax.broadcasted_iota(jnp.int32, (QB, QB), 1)
        power = jnp.where(past, table_ref[i : i + 1, :] - wide(top, QB), NEG)
        den_ref[here, :], num_ref[here, :] = sums(i, jnp.exp(power) * scores(i))

        def earlier(m, shift):
            j = i - 1 - m
            shift = shift + table_ref[pl.ds(BLOCKS + j, 1), :][:, QB - 1 :]
            reach = table_ref[pl.ds(j, 1), :]
            peak = jnp.max(reach, axis=1, keepdims=True)
            lanes, product = sums(j, scores(j) * jnp.exp(reach - peak))
            factor = jnp.exp((peak + shift) - top)
            den_ref[here, :] += factor * lanes
            num_ref[here, :] += wide(factor, DV) * product
            return shift

        if i:
            lax.fori_loop(0, i, earlier, jnp.zeros((1, 1), F32))


def first_kernel(blocks, g_ref, tick_ref, q_hbm, k_hbm, v_ref, num_ref, den_ref, table_ref, q_ref, k_ref, q_sem, k_sem):
    copies = [pltpu.make_async_copy(q_hbm, q_ref, q_sem), pltpu.make_async_copy(k_hbm, k_ref, k_sem)]
    for copy in copies:
        copy.start()
    tables(g_ref, table_ref)
    for copy in copies:
        copy.wait()
    local_kernel(blocks, table_ref, tick_ref, q_ref, k_ref, v_ref, num_ref, den_ref)


def local(blocks, gates, tick, queries, keys, values, table=None):
    count = len(blocks)
    units = sum(blocks) + count
    first = table is None
    out_shape = [
        jax.ShapeDtypeStruct((count * QB, DV), F32),
        jax.ShapeDtypeStruct((count * QB, LANES), F32),
        jax.ShapeDtypeStruct((3 * BLOCKS, QB), F32),
        jax.ShapeDtypeStruct((TOKS, DQK), BF16),
        jax.ShapeDtypeStruct((TOKS, DQK), BF16),
    ][: 5 if first else 2]
    return pl.pallas_call(
        functools.partial(first_kernel if first else local_kernel, blocks),
        in_specs=[VMEM, ANY, HBM, HBM, VMEM] if first else [VMEM, ANY] + [VMEM] * 3,
        out_specs=[VMEM] * len(out_shape),
        out_shape=out_shape,
        scratch_shapes=[pltpu.SemaphoreType.DMA(())] * (2 * first),
        compiler_params=pltpu.CompilerParams(vmem_limit_bytes=8 * MIB),
        cost_estimate=pl.CostEstimate(flops=800_000_000 * units, bytes_accessed=MIB * units, transcendentals=0),
        name="within_shard",
    )(*((gates, tick, in_hbm(queries), in_hbm(keys), values) if first else (table, tick, queries, keys, values)))


def scale_kernel(table_ref, mine_ref, q_ref, total_ref, got_ref, *refs):
    dens, (kept_ref, carried_ref, close_ref, norm_ref, top_ref) = refs[:-5], refs[-5:]
    z = place_of("ctx_0")
    later = later_of(z, 2)
    here = pl.ds(pl.multiple_of(z * ROWS, ROWS), ROWS)
    own, got = pieces_of(total_ref[SLICE:, :]), pieces_of(got_ref[SLICE:, :])
    first = [jnp.where(later, g, o) for g, o in zip(got, own)]
    second = [jnp.where(later, o, g) for g, o in zip(got, own)]
    keep, take, (end_norm, end_top, _) = chain_of(first, second)
    f_own, f_got = jnp.where(later, take, keep), jnp.where(later, keep, take)
    close_ref[0] = f_own * total_ref[here, :] + f_got * got_ref[here, :]
    norm_ref[...] = end_norm[:, :DQK]
    top_ref[...] = end_top[:, :LANES]
    norm, log_in, _ = pieces_of(mine_ref)
    norm, log_in = norm[:, :DQK], log_in[:, :LANES]
    place = {i: (dens[n], m) for n, blocks in enumerate(PARTS) for m, i in enumerate(blocks)}
    for i in range(BLOCKS):
        den_ref, m = place[i]
        here, there = pl.ds(i * QB, QB), pl.ds(m * QB, QB)
        top = column(table_ref[2 * BLOCKS + i : 2 * BLOCKS + i + 1, :])
        peak = jnp.maximum(top, log_in)
        kept, carried = jnp.exp(top - peak) * (DQK**-0.5), jnp.exp(log_in - peak)
        from_norm = jnp.sum(q_ref[here, :].astype(F32) * norm, axis=1, keepdims=True)
        denom = jnp.sum(den_ref[there, :], axis=1, keepdims=True) * kept + carried * from_norm
        inverse = 1.0 / jnp.maximum(jnp.abs(denom), 1.0)
        kept_ref[here, :] = kept * inverse
        carried_ref[here, :] = carried * inverse
        log_in = log_in + table_ref[BLOCKS + i : BLOCKS + i + 1, :][:, QB - 1 :]


def scales(table, mine, queries, total, got, dens):
    return pl.pallas_call(
        scale_kernel,
        in_specs=[VMEM] * (5 + len(dens)),
        out_specs=[VMEM] * 5,
        out_shape=[jax.ShapeDtypeStruct((TOKS, LANES), F32)] * 2
        + [
            jax.ShapeDtypeStruct((1, ROWS, DV), F32),
            jax.ShapeDtypeStruct((1, DQK), F32),
            jax.ShapeDtypeStruct((1, LANES), F32),
        ],
        compiler_params=pltpu.CompilerParams(vmem_limit_bytes=4 * MIB),
        cost_estimate=pl.CostEstimate(flops=600_000_000, bytes_accessed=4 * MIB, transcendentals=0),
        name="row_scales",
    )(table, mine, queries, total, got, *dens)


def joined_kernel(q_ref, own_ref, one_ref, two_ref, three_ref, kept_ref, carried_ref, *refs):
    nums, (out_hbm, mem_ref, mem_b_ref, out_ref, sem) = refs[:-5], refs[-5:]
    x = place_of("ctx_1")
    for k, ref in enumerate((own_ref, one_ref, two_ref, three_ref)):
        at = lax.rem(x + XS - k, XS)
        mem_ref[:, pl.ds(at, 1)] = ref[...].reshape(ZS, 1, ROWS, DV)
    mem_b_ref[...] = mem_ref[...].reshape(DQK, DV).astype(BF16)
    copies = []
    for n, blocks in enumerate(PARTS):
        for m, i in enumerate(blocks):
            for half in range(0, QB, PIECE):
                span, there = pl.ds(i * QB + half, PIECE), pl.ds(m * QB + half, PIECE)
                product = jnp.dot(q_ref[span, :], mem_b_ref[...], preferred_element_type=F32)
                local_part = wide(kept_ref[span, :], DV) * nums[n][there, :]
                out_ref[span, :] = (local_part + wide(carried_ref[span, :], DV) * product).astype(BF16)
                copies.append(pltpu.make_async_copy(out_ref.at[span], out_hbm.at[span], sem.at[len(copies)]))
                copies[-1].start()
    for copy in copies:
        copy.wait()


def joined(queries, parts, kept, carried, nums):
    return pl.pallas_call(
        joined_kernel,
        in_specs=[VMEM] * (7 + len(nums)),
        out_specs=HBM,
        out_shape=jax.ShapeDtypeStruct((TOKS, DV), BF16),
        scratch_shapes=[
            pltpu.VMEM((ZS, XS, ROWS, DV), F32),
            pltpu.VMEM((DQK, DV), BF16),
            pltpu.VMEM((TOKS, DV), BF16),
            pltpu.SemaphoreType.DMA((PIECES,)),
        ],
        compiler_params=pltpu.CompilerParams(vmem_limit_bytes=8 * MIB),
        cost_estimate=pl.CostEstimate(flops=600_000_000, bytes_accessed=9 * MIB, transcendentals=0),
        name="join_memory",
    )(queries, *parts, kept, carried, *nums)


def exchanged(x, axis):
    return lax.all_to_all(x, axis, split_axis=0, concat_axis=0, tiled=True)


def around(parts):
    moved = [parts[0]]
    for k in range(1, XS):
        moved.append(lax.ppermute(parts[k], "ctx_1", [(i, (i + k) % XS) for i in range(XS)]))
    return moved


def swapped(x, partner):
    return lax.ppermute(x, "ctx_0", [(i, partner(i)) for i in range(ZS)])


def on_device(queries, keys, values, gate_pre):
    gates = exchanged(gate_sums(gate_pre), "head")
    keys_t, values = turned(keys, values)
    *parts, tick = state(gates, keys_t, values)
    moved = around(parts)
    num_a, den_a, table, queries, keys = local(PARTS[0], gates, tick, queries, keys, values)
    qkv = (queries, keys, values)
    total, everything = grouped(moved, den_a)
    got = swapped(total, lambda i: i ^ 1)
    total, prefix = round_of(first_round_kernel, total, got, den_a)
    got = swapped(total, lambda i: i ^ 2)
    num_b, den_b = local(PARTS[1], None, prefix, *qkv, table)
    total, prefix = round_of(next_round_kernel, total, got, prefix, den_b)
    got = swapped(total, lambda i: (6, 7, 5, 4, 3, 2, 0, 1)[i])
    num_c, den_c = local(PARTS[2], None, prefix, *qkv, table)
    *parts, mine = spread(got, prefix, everything, den_c)
    moved = around(parts)
    kept, carried, closing, final_norm, top = scales(table, mine, queries, total, got, [den_a, den_b, den_c])
    hidden = joined(queries, moved, kept, carried, [num_a, num_b, num_c])
    return (hidden, closing, final_norm, top[0, :1])


def solution(mesh):
    split = Mesh(mesh.devices.reshape(8, 4, mesh.shape["head"]), ("ctx_0", "ctx_1", "head"))
    in_specs = (P(CTX, "head"), P(CTX, "head"), P(CTX, "head"), P(None, None, CTX_HEAD))
    out_specs = (P(CTX, "head"), P("head", CTX, None), P("head", None), P("head"))
    return jax.shard_map(
        on_device, mesh=split, in_specs=in_specs, out_specs=out_specs, check_vma=False
    )
```

```python
import functools

import jax
import jax.numpy as jnp
from jax import lax
from jax.experimental import pallas as pl
from jax.experimental.pallas import tpu as pltpu
from jax.sharding import Mesh
from jax.sharding import PartitionSpec as P

DQK = 256
DV = 512
XS = 4
ZS = 8
ROWS = DQK // (XS * ZS)
PIECES = 8
PIECE = 256
LANES = 128
SLICE = ZS * DV
SENT = SLICE + LANES
TOKS = PIECES * PIECE
QB = 512
BLOCKS = TOKS // QB
PARTS = ((3,), (0, 1), (2,))
CTX = ("ctx_0", "ctx_1")
CTX_HEAD = ("ctx_0", "ctx_1", "head")
NEG = -1e30
F32 = jnp.float32
BF16 = jnp.bfloat16
VMEM = pl.BlockSpec(memory_space=pltpu.VMEM)
HBM = pl.BlockSpec(memory_space=pltpu.HBM)
ANY = pl.BlockSpec(memory_space=pl.ANY)
MIB = 1 << 20


def in_hbm(x):
    return pltpu.with_memory_space_constraint(x, pltpu.HBM)


def place_of(axis):
    return lax.axis_index(axis).astype(jnp.int32)


def log_sigmoid(x):
    z = jnp.exp(-jnp.abs(x))
    s = z / (2.0 + z)
    s2 = s * s
    tail = jnp.full_like(s, 1.0 / 17.0)
    for n in (15, 13, 11, 9, 7, 5, 3, 1):
        tail = tail * s2 + 1.0 / n
    return jnp.minimum(x, 0.0) - 2.0 * s * tail


def three_parts(x):
    high = x.astype(BF16)
    rest = x - high.astype(F32)
    mid = rest.astype(BF16)
    low = (rest - mid.astype(F32)).astype(BF16)
    return high, mid, low


def piece_sums(forget):
    n = forget.shape[1]
    upto = lax.broadcasted_iota(jnp.int32, (n, n), 0) <= lax.broadcasted_iota(jnp.int32, (n, n), 1)
    ones = jnp.where(upto, 1.0, 0.0).astype(BF16)
    parts = jnp.concatenate([p.astype(F32) for p in three_parts(log_sigmoid(forget))], axis=0)
    sums = jnp.dot(parts.astype(BF16), ones, preferred_element_type=F32)
    k = forget.shape[0]
    return sums[:k] + sums[k : 2 * k] + sums[2 * k :]


def gate_kernel(g_hbm, out_ref, g_ref, sem):
    copy = pltpu.make_async_copy(g_hbm, g_ref, sem)
    copy.start()
    copy.wait()
    cum = piece_sums(g_ref[1])
    own = g_ref[0] - cum
    for h in range(own.shape[0]):
        out_ref[h, 0:1, :] = own[h : h + 1]
        out_ref[h, 1:2, :] = cum[h : h + 1]


def gate_sums(gate_pre):
    kinds, heads, n = gate_pre.shape
    return pl.pallas_call(
        gate_kernel,
        in_specs=[HBM],
        out_specs=VMEM,
        out_shape=jax.ShapeDtypeStruct((heads, kinds, n), F32),
        scratch_shapes=[pltpu.VMEM(gate_pre.shape, F32), pltpu.SemaphoreType.DMA(())],
        compiler_params=pltpu.CompilerParams(vmem_limit_bytes=4 * MIB),
        name="gate_sums",
    )(in_hbm(gate_pre))


def turned_kernel(k_hbm, v_hbm, kt_ref, v_ref, k_ref, k_sem, v_sem):
    copies = []
    for j in range(BLOCKS):
        span = pl.ds(j * QB, QB)
        copies.append(pltpu.make_async_copy(k_hbm.at[span], k_ref.at[span], k_sem.at[j]))
        copies[-1].start()
    values = pltpu.make_async_copy(v_hbm, v_ref, v_sem)
    values.start()
    for j in range(BLOCKS):
        span = pl.ds(j * QB, QB)
        copies[j].wait()
        kt_ref[:, span] = k_ref[span, :].T
    values.wait()


def turned(keys, values):
    return pl.pallas_call(
        turned_kernel,
        in_specs=[HBM] * 2,
        out_specs=[VMEM] * 2,
        out_shape=[jax.ShapeDtypeStruct((DQK, TOKS), BF16), jax.ShapeDtypeStruct((TOKS, DV), BF16)],
        scratch_shapes=[
            pltpu.VMEM((TOKS, DQK), BF16),
            pltpu.SemaphoreType.DMA((BLOCKS,)),
            pltpu.SemaphoreType.DMA(()),
        ],
        compiler_params=pltpu.CompilerParams(vmem_limit_bytes=4 * MIB),
        cost_estimate=pl.CostEstimate(flops=0, bytes_accessed=4 * MIB, transcendentals=0),
        name="turn_keys",
    )(in_hbm(keys), in_hbm(values))


def state_kernel(g_ref, kt_ref, v_ref, own_ref, one_ref, two_ref, three_ref, tick_ref, w_ref, acc_ref):
    own = g_ref[:, 0, :]
    cum = g_ref[:, 1, :]
    later = jnp.broadcast_to(cum[:, PIECE - 1 :], cum.shape)
    row = lax.broadcasted_iota(jnp.int32, cum.shape, 0)
    for shift in (1, 2, 4):
        moved = pltpu.roll(later, PIECES - shift, 0)
        later = later + jnp.where(row + shift < PIECES, moved, 0.0)
    reach = own + later
    stab = jnp.max(jnp.max(reach, axis=1, keepdims=True), axis=0, keepdims=True)
    w_ref[...] = jnp.exp(reach - stab) * (DQK**-0.5)
    norm = jnp.zeros((24, DQK), F32)
    for j in range(BLOCKS):
        span = pl.ds(j * QB, QB)
        weight = jnp.concatenate([w_ref[2 * j : 2 * j + 1, :], w_ref[2 * j + 1 : 2 * j + 2, :]], axis=1)
        k = kt_ref[:, span]
        scaled = (k.astype(F32) * weight).astype(BF16)
        parts = [jnp.broadcast_to(p.astype(F32), (8, QB)) for p in three_parts(weight)]
        parts = jnp.concatenate(parts, axis=0).astype(BF16)
        norm += lax.dot_general(parts, k, (((1,), (1,)), ((), ())), preferred_element_type=F32)
        product = jnp.dot(scaled, v_ref[span, :], preferred_element_type=F32)
        if j:
            product += acc_ref[...].reshape(DQK, DV)
        acc_ref[...] = product.reshape(ZS, XS, ROWS, DV)
    norm = norm[0:8] + norm[8:16] + norm[16:24]
    norm = jnp.concatenate([norm[0:1, :LANES], norm[0:1, LANES:]], axis=0)
    extra = tail_of(norm, stab, later[0:1, :LANES])
    x = place_of("ctx_1")
    for k, ref in enumerate((own_ref, one_ref, two_ref, three_ref)):
        to = lax.rem(x + k, XS)
        for z in range(ZS):
            ref[:, z * DV : (z + 1) * DV] = acc_ref[z, pl.ds(to, 1)].reshape(ROWS, DV)
        ref[:, SLICE:] = extra
    tick_ref[...] = extra


def state(gates, keys_t, values):
    return pl.pallas_call(
        state_kernel,
        in_specs=[VMEM, VMEM, VMEM],
        out_specs=[VMEM] * 5,
        out_shape=[jax.ShapeDtypeStruct((ROWS, SENT), F32)] * 4 + [jax.ShapeDtypeStruct((8, LANES), F32)],
        scratch_shapes=[
            pltpu.VMEM((PIECES, PIECE), F32),
            pltpu.VMEM((ZS, XS, ROWS, DV), F32),
        ],
        compiler_params=pltpu.CompilerParams(vmem_limit_bytes=12 * MIB),
        cost_estimate=pl.CostEstimate(flops=600_000_000, bytes_accessed=5 * MIB, transcendentals=0),
        name="shard_state",
    )(gates, keys_t, values)


def tail_of(norm, stab, total):
    row = lax.broadcasted_iota(jnp.int32, (8, LANES), 0)
    tail = jnp.where(row == 0, norm[0:1], norm[1:2])
    return jnp.where(row == 2, stab, jnp.where(row == 3, total, tail))


def pieces_of(tail):
    return tail[0:2, :], tail[2:3, :], tail[3:4, :]


def chain_of(early, late):
    norm_e, stab_e, total_e = early
    norm_l, stab_l, total_l = late
    shifted = stab_e + total_l
    stab = jnp.maximum(shifted, stab_l)
    keep, take = jnp.exp(shifted - stab), jnp.exp(stab_l - stab)
    return keep, take, (keep * norm_e + take * norm_l, stab, total_e + total_l)


def spans():
    return [slice(z * DV, (z + 1) * DV) for z in range(ZS)]


def group_kernel(own_ref, one_ref, two_ref, three_ref, after_ref, out_ref, all_ref):
    x = place_of("ctx_1")
    for k, ref in enumerate((own_ref, one_ref, two_ref, three_ref)):
        at = lax.rem(x + XS - k, XS)
        all_ref[pl.ds(at, 1)] = ref[...].reshape(1, ROWS, SENT)
    small = pieces_of(all_ref[0, :, SLICE:])
    factors = []
    for j in range(1, XS):
        keep, take, small = chain_of(small, pieces_of(all_ref[j, :, SLICE:]))
        factors.append((wide(keep, DV), wide(take, DV)))
    for here in spans():
        memory = all_ref[0, :, here]
        for j, (keep, take) in enumerate(factors):
            memory = keep * memory + take * all_ref[j + 1, :, here]
        out_ref[:, here] = memory
    out_ref[:, SLICE:] = tail_of(*small)


def grouped(parts, after):
    return pl.pallas_call(
        group_kernel,
        in_specs=[VMEM] * 4 + [ANY],
        out_specs=[VMEM] * 2,
        out_shape=[
            jax.ShapeDtypeStruct((ROWS, SENT), F32),
            jax.ShapeDtypeStruct((XS, ROWS, SENT), F32),
        ],
        compiler_params=pltpu.CompilerParams(vmem_limit_bytes=4 * MIB),
        cost_estimate=pl.CostEstimate(flops=1_000_000, bytes_accessed=2 * MIB, transcendentals=0),
        name="group_states",
    )(*parts, after)


def merged(later, total_ref, got_ref):
    own, got = pieces_of(total_ref[:, SLICE:]), pieces_of(got_ref[:, SLICE:])
    first = [jnp.where(later, g, o) for g, o in zip(got, own)]
    second = [jnp.where(later, o, g) for g, o in zip(got, own)]
    keep, take, small = chain_of(first, second)
    return wide(jnp.where(later, take, keep), DV), wide(jnp.where(later, keep, take), DV), small


def brought(later, got_ref, before):
    bring, hold, small = chain_of(pieces_of(got_ref[:, SLICE:]), before)
    bring, hold = jnp.where(later, bring, 0.0), jnp.where(later, hold, 1.0)
    return wide(bring, DV), wide(hold, DV), [jnp.where(later, n, o) for n, o in zip(small, before)]


def later_of(z, bit):
    return lax.rem(lax.div(z, 1 << bit), 2) == 1


def first_round_kernel(total_ref, got_ref, after_ref, new_total, new_prefix):
    later = later_of(place_of("ctx_0"), 0)
    f_own, f_got, total = merged(later, total_ref, got_ref)
    nothing = (jnp.zeros((2, LANES), F32), jnp.full((1, LANES), NEG, F32), jnp.zeros((1, LANES), F32))
    bring, _, prefix = brought(later, got_ref, nothing)
    for here in spans():
        new_total[:, here] = f_own * total_ref[:, here] + f_got * got_ref[:, here]
        new_prefix[:, here] = bring * got_ref[:, here]
    new_total[:, SLICE:] = tail_of(*total)
    new_prefix[:, SLICE:] = tail_of(*prefix)


def next_round_kernel(total_ref, got_ref, prefix_ref, after_ref, new_total, new_prefix):
    later = later_of(place_of("ctx_0"), 1)
    f_own, f_got, total = merged(later, total_ref, got_ref)
    bring, hold, prefix = brought(later, got_ref, pieces_of(prefix_ref[:, SLICE:]))
    for here in spans():
        new_total[:, here] = f_own * total_ref[:, here] + f_got * got_ref[:, here]
        new_prefix[:, here] = bring * got_ref[:, here] + hold * prefix_ref[:, here]
    new_total[:, SLICE:] = tail_of(*total)
    new_prefix[:, SLICE:] = tail_of(*prefix)


def round_of(kernel, *args):
    return pl.pallas_call(
        kernel,
        in_specs=[VMEM] * (len(args) - 1) + [ANY],
        out_specs=[VMEM] * 2,
        out_shape=[jax.ShapeDtypeStruct((ROWS, SENT), F32)] * 2,
        compiler_params=pltpu.CompilerParams(vmem_limit_bytes=4 * MIB),
        cost_estimate=pl.CostEstimate(flops=1_000_000, bytes_accessed=MIB, transcendentals=0),
        name="merge_round",
    )(*args)


def spread_kernel(got_ref, prefix_ref, all_ref, after_ref, own_ref, one_ref, two_ref, three_ref, mine_ref, out_ref):
    x = place_of("ctx_1")
    later = later_of(place_of("ctx_0"), 2)
    bring, hold, small = brought(later, got_ref, pieces_of(prefix_ref[:, SLICE:]))
    mine = small
    factors = []
    for j in range(XS - 1):
        keep, take, small = chain_of(small, pieces_of(all_ref[j, :, SLICE:]))
        mine = [jnp.where(x == j + 1, n, o) for n, o in zip(small, mine)]
        factors.append((wide(keep, DV), wide(take, DV)))
    for z, here in enumerate(spans()):
        memory = bring * got_ref[:, here] + hold * prefix_ref[:, here]
        out_ref[0, z] = memory
        for j, (keep, take) in enumerate(factors):
            memory = keep * memory + take * all_ref[j, :, here]
            out_ref[j + 1, z] = memory
    for k, ref in enumerate((own_ref, one_ref, two_ref, three_ref)):
        ref[...] = out_ref[pl.ds(lax.rem(x + k, XS), 1)].reshape(ZS, ROWS, DV)
    mine_ref[...] = tail_of(*mine)


def spread(got, prefix, everything, after):
    return pl.pallas_call(
        spread_kernel,
        in_specs=[VMEM] * 3 + [ANY],
        out_specs=[VMEM] * 5,
        out_shape=[jax.ShapeDtypeStruct((ZS, ROWS, DV), F32)] * 4 + [jax.ShapeDtypeStruct((8, LANES), F32)],
        scratch_shapes=[pltpu.VMEM((XS, ZS, ROWS, DV), F32)],
        compiler_params=pltpu.CompilerParams(vmem_limit_bytes=4 * MIB),
        cost_estimate=pl.CostEstimate(flops=1_000_000, bytes_accessed=2 * MIB, transcendentals=0),
        name="spread_prefixes",
    )(got, prefix, everything, after)


def wide(x, n):
    return jnp.concatenate([x] * (n // LANES), axis=1)


def column(row):
    n = row.shape[1]
    return jnp.concatenate(
        [
            jnp.broadcast_to(row[:, at : at + LANES], (LANES, LANES)).T
            for at in range(0, n, LANES)
        ],
        axis=0,
    )


def tables(g_ref, table_ref):
    own, cum = [], []
    for r in range(0, PIECES, 2):
        first = g_ref[r, 1:2, :][:, PIECE - 1 :]
        own.append(jnp.concatenate([g_ref[r, 0:1, :], g_ref[r + 1, 0:1, :] - first], axis=1))
        cum.append(jnp.concatenate([g_ref[r, 1:2, :], g_ref[r + 1, 1:2, :] + first], axis=1))
    own = jnp.concatenate(own, axis=0)
    cum = jnp.concatenate(cum, axis=0)
    table_ref[0:BLOCKS, :] = own
    table_ref[BLOCKS : 2 * BLOCKS, :] = cum
    lane = lax.broadcasted_iota(jnp.int32, (BLOCKS, QB), 1)
    top = own
    shift = 1
    while shift < QB:
        moved = pltpu.roll(top, shift, 1)
        top = jnp.maximum(top, jnp.where(lane >= shift, moved, NEG))
        shift *= 2
    stab = jnp.full((1, 1), NEG, F32)
    for r in range(BLOCKS):
        at = 2 * BLOCKS + r
        table_ref[at : at + 1, :] = jnp.maximum(top[r : r + 1], stab)
        stab = jnp.maximum(stab, top[r : r + 1, QB - 1 :]) + cum[r : r + 1, QB - 1 :]


def local_kernel(blocks, table_ref, tick_ref, q_ref, k_ref, v_ref, num_ref, den_ref):
    for n, i in enumerate(blocks):
        here = pl.ds(n * QB, QB)
        top = column(table_ref[2 * BLOCKS + i : 2 * BLOCKS + i + 1, :])
        q = q_ref[pl.ds(i * QB, QB), :]

        def scores(j):
            at = pl.ds(pl.multiple_of(j * QB, QB), QB)
            return lax.dot_general(q, k_ref[at, :], (((1,), (1,)), ((), ())), preferred_element_type=F32)

        def sums(j, mixed):
            at = pl.ds(pl.multiple_of(j * QB, QB), QB)
            lanes = sum(mixed[:, c : c + LANES] for c in range(0, QB, LANES))
            return lanes, jnp.dot(mixed.astype(BF16), v_ref[at, :], preferred_element_type=F32)

        past = lax.broadcasted_iota(jnp.int32, (QB, QB), 0) >= lax.broadcasted_iota(jnp.int32, (QB, QB), 1)
        power = jnp.where(past, table_ref[i : i + 1, :] - wide(top, QB), NEG)
        den_ref[here, :], num_ref[here, :] = sums(i, jnp.exp(power) * scores(i))

        def earlier(m, shift):
            j = i - 1 - m
            shift = shift + table_ref[pl.ds(BLOCKS + j, 1), :][:, QB - 1 :]
            reach = table_ref[pl.ds(j, 1), :]
            peak = jnp.max(reach, axis=1, keepdims=True)
            lanes, product = sums(j, scores(j) * jnp.exp(reach - peak))
            factor = jnp.exp((peak + shift) - top)
            den_ref[here, :] += factor * lanes
            num_ref[here, :] += wide(factor, DV) * product
            return shift

        if i:
            lax.fori_loop(0, i, earlier, jnp.zeros((1, 1), F32))


def first_kernel(blocks, g_ref, tick_ref, q_hbm, k_hbm, v_ref, num_ref, den_ref, table_ref, q_ref, k_ref, q_sem, k_sem):
    copies = [pltpu.make_async_copy(q_hbm, q_ref, q_sem), pltpu.make_async_copy(k_hbm, k_ref, k_sem)]
    for copy in copies:
        copy.start()
    tables(g_ref, table_ref)
    for copy in copies:
        copy.wait()
    local_kernel(blocks, table_ref, tick_ref, q_ref, k_ref, v_ref, num_ref, den_ref)


def local(blocks, gates, tick, queries, keys, values, table=None):
    count = len(blocks)
    units = sum(blocks) + count
    first = table is None
    out_shape = [
        jax.ShapeDtypeStruct((count * QB, DV), F32),
        jax.ShapeDtypeStruct((count * QB, LANES), F32),
        jax.ShapeDtypeStruct((3 * BLOCKS, QB), F32),
        jax.ShapeDtypeStruct((TOKS, DQK), BF16),
        jax.ShapeDtypeStruct((TOKS, DQK), BF16),
    ][: 5 if first else 2]
    return pl.pallas_call(
        functools.partial(first_kernel if first else local_kernel, blocks),
        in_specs=[VMEM, ANY, HBM, HBM, VMEM] if first else [VMEM, ANY] + [VMEM] * 3,
        out_specs=[VMEM] * len(out_shape),
        out_shape=out_shape,
        scratch_shapes=[pltpu.SemaphoreType.DMA(())] * (2 * first),
        compiler_params=pltpu.CompilerParams(vmem_limit_bytes=8 * MIB),
        cost_estimate=pl.CostEstimate(flops=800_000_000 * units, bytes_accessed=MIB * units, transcendentals=0),
        name="within_shard",
    )(*((gates, tick, in_hbm(queries), in_hbm(keys), values) if first else (table, tick, queries, keys, values)))


def scale_kernel(table_ref, mine_ref, q_ref, total_ref, got_ref, *refs):
    dens, (kept_ref, carried_ref, close_ref, norm_ref, top_ref) = refs[:-5], refs[-5:]
    z = place_of("ctx_0")
    here = pl.ds(pl.multiple_of(z * DV, DV), DV)
    f_own, f_got, (end_norm, end_top, _) = merged(later_of(z, 2), total_ref, got_ref)
    close_ref[0] = f_own * total_ref[:, here] + f_got * got_ref[:, here]
    norm_ref[:, :LANES] = end_norm[0:1]
    norm_ref[:, LANES:] = end_norm[1:2]
    top_ref[...] = end_top
    norm, log_in, _ = pieces_of(mine_ref)
    norm = jnp.concatenate([norm[0:1], norm[1:2]], axis=1)
    place = {i: (dens[n], m) for n, blocks in enumerate(PARTS) for m, i in enumerate(blocks)}
    for i in range(BLOCKS):
        den_ref, m = place[i]
        here, there = pl.ds(i * QB, QB), pl.ds(m * QB, QB)
        top = column(table_ref[2 * BLOCKS + i : 2 * BLOCKS + i + 1, :])
        peak = jnp.maximum(top, log_in)
        kept, carried = jnp.exp(top - peak) * (DQK**-0.5), jnp.exp(log_in - peak)
        from_norm = jnp.sum(q_ref[here, :].astype(F32) * norm, axis=1, keepdims=True)
        denom = jnp.sum(den_ref[there, :], axis=1, keepdims=True) * kept + carried * from_norm
        inverse = 1.0 / jnp.maximum(jnp.abs(denom), 1.0)
        kept_ref[here, :] = kept * inverse
        carried_ref[here, :] = carried * inverse
        log_in = log_in + table_ref[BLOCKS + i : BLOCKS + i + 1, :][:, QB - 1 :]


def scales(table, mine, queries, total, got, dens):
    return pl.pallas_call(
        scale_kernel,
        in_specs=[VMEM] * (5 + len(dens)),
        out_specs=[VMEM] * 5,
        out_shape=[jax.ShapeDtypeStruct((TOKS, LANES), F32)] * 2
        + [
            jax.ShapeDtypeStruct((1, ROWS, DV), F32),
            jax.ShapeDtypeStruct((1, DQK), F32),
            jax.ShapeDtypeStruct((1, LANES), F32),
        ],
        compiler_params=pltpu.CompilerParams(vmem_limit_bytes=4 * MIB),
        cost_estimate=pl.CostEstimate(flops=600_000_000, bytes_accessed=4 * MIB, transcendentals=0),
        name="row_scales",
    )(table, mine, queries, total, got, *dens)


def joined_kernel(q_ref, own_ref, one_ref, two_ref, three_ref, kept_ref, carried_ref, *refs):
    nums, (out_hbm, mem_ref, mem_b_ref, out_ref, sem) = refs[:-5], refs[-5:]
    x = place_of("ctx_1")
    for k, ref in enumerate((own_ref, one_ref, two_ref, three_ref)):
        at = lax.rem(x + XS - k, XS)
        mem_ref[:, pl.ds(at, 1)] = ref[...].reshape(ZS, 1, ROWS, DV)
    mem_b_ref[...] = mem_ref[...].reshape(DQK, DV).astype(BF16)
    copies = []
    for n, blocks in enumerate(PARTS):
        for m, i in enumerate(blocks):
            for half in range(0, QB, PIECE):
                span, there = pl.ds(i * QB + half, PIECE), pl.ds(m * QB + half, PIECE)
                product = jnp.dot(q_ref[span, :], mem_b_ref[...], preferred_element_type=F32)
                local_part = wide(kept_ref[span, :], DV) * nums[n][there, :]
                out_ref[span, :] = (local_part + wide(carried_ref[span, :], DV) * product).astype(BF16)
                copies.append(pltpu.make_async_copy(out_ref.at[span], out_hbm.at[span], sem.at[len(copies)]))
                copies[-1].start()
    for copy in copies:
        copy.wait()


def joined(queries, parts, kept, carried, nums):
    return pl.pallas_call(
        joined_kernel,
        in_specs=[VMEM] * (7 + len(nums)),
        out_specs=HBM,
        out_shape=jax.ShapeDtypeStruct((TOKS, DV), BF16),
        scratch_shapes=[
            pltpu.VMEM((ZS, XS, ROWS, DV), F32),
            pltpu.VMEM((DQK, DV), BF16),
            pltpu.VMEM((TOKS, DV), BF16),
            pltpu.SemaphoreType.DMA((PIECES,)),
        ],
        compiler_params=pltpu.CompilerParams(vmem_limit_bytes=8 * MIB),
        cost_estimate=pl.CostEstimate(flops=600_000_000, bytes_accessed=9 * MIB, transcendentals=0),
        name="join_memory",
    )(queries, *parts, kept, carried, *nums)


def exchanged(x, axis):
    return lax.all_to_all(x, axis, split_axis=0, concat_axis=0, tiled=True)


def around(parts):
    moved = [parts[0]]
    for k in range(1, XS):
        moved.append(lax.ppermute(parts[k], "ctx_1", [(i, (i + k) % XS) for i in range(XS)]))
    return moved


def swapped(x, partner):
    return lax.ppermute(x, "ctx_0", [(i, partner(i)) for i in range(ZS)])


def on_device(queries, keys, values, gate_pre):
    gates = exchanged(gate_sums(gate_pre), "head")
    keys_t, values = turned(keys, values)
    *parts, tick = state(gates, keys_t, values)
    moved = around(parts)
    num_a, den_a, table, queries, keys = local(PARTS[0], gates, tick, queries, keys, values)
    qkv = (queries, keys, values)
    total, everything = grouped(moved, den_a)
    got = swapped(total, lambda i: i ^ 1)
    total, prefix = round_of(first_round_kernel, total, got, den_a)
    got = swapped(total, lambda i: i ^ 2)
    num_b, den_b = local(PARTS[1], None, prefix, *qkv, table)
    total, prefix = round_of(next_round_kernel, total, got, prefix, den_b)
    got = swapped(total, lambda i: (6, 7, 5, 4, 3, 2, 0, 1)[i])
    num_c, den_c = local(PARTS[2], None, prefix, *qkv, table)
    *parts, mine = spread(got, prefix, everything, den_c)
    moved = around(parts)
    kept, carried, closing, final_norm, top = scales(table, mine, queries, total, got, [den_a, den_b, den_c])
    hidden = joined(queries, moved, kept, carried, [num_a, num_b, num_c])
    return (hidden, closing, final_norm, top[0, :1])


def solution(mesh):
    split = Mesh(mesh.devices.reshape(8, 4, mesh.shape["head"]), ("ctx_0", "ctx_1", "head"))
    in_specs = (P(CTX, "head"), P(CTX, "head"), P(CTX, "head"), P(None, None, CTX_HEAD))
    out_specs = (P(CTX, "head"), P("head", CTX, None), P("head", None), P("head"))
    return jax.shard_map(
        on_device, mesh=split, in_specs=in_specs, out_specs=out_specs, check_vma=False
    )
```

```python
import functools

import jax
import jax.numpy as jnp
from jax import lax
from jax.experimental import pallas as pl
from jax.experimental.pallas import tpu as pltpu
from jax.sharding import Mesh
from jax.sharding import PartitionSpec as P

DQK = 256
DV = 512
XS = 4
ZS = 8
ROWS = DQK // (XS * ZS)
PIECES = 8
PIECE = 256
LANES = 128
SLICE = ZS * DV
SENT = SLICE + LANES
TOKS = PIECES * PIECE
QB = 512
BLOCKS = TOKS // QB
PARTS = ((3,), (0, 1), (2,))
CTX = ("ctx_0", "ctx_1")
CTX_HEAD = ("ctx_0", "ctx_1", "head")
NEG = -1e30
F32 = jnp.float32
BF16 = jnp.bfloat16
VMEM = pl.BlockSpec(memory_space=pltpu.VMEM)
HBM = pl.BlockSpec(memory_space=pltpu.HBM)
ANY = pl.BlockSpec(memory_space=pl.ANY)
MIB = 1 << 20


def in_hbm(x):
    return pltpu.with_memory_space_constraint(x, pltpu.HBM)


def place_of(axis):
    return lax.axis_index(axis).astype(jnp.int32)


def log_sigmoid(x):
    z = jnp.exp(-jnp.abs(x))
    s = z / (2.0 + z)
    s2 = s * s
    tail = jnp.full_like(s, 1.0 / 17.0)
    for n in (15, 13, 11, 9, 7, 5, 3, 1):
        tail = tail * s2 + 1.0 / n
    return jnp.minimum(x, 0.0) - 2.0 * s * tail


def three_parts(x):
    high = x.astype(BF16)
    rest = x - high.astype(F32)
    mid = rest.astype(BF16)
    low = (rest - mid.astype(F32)).astype(BF16)
    return high, mid, low


def piece_sums(forget):
    n = forget.shape[1]
    upto = lax.broadcasted_iota(jnp.int32, (n, n), 0) <= lax.broadcasted_iota(jnp.int32, (n, n), 1)
    ones = jnp.where(upto, 1.0, 0.0).astype(BF16)
    parts = jnp.concatenate([p.astype(F32) for p in three_parts(log_sigmoid(forget))], axis=0)
    sums = jnp.dot(parts.astype(BF16), ones, preferred_element_type=F32)
    k = forget.shape[0]
    return sums[:k] + sums[k : 2 * k] + sums[2 * k :]


def gate_kernel(g_hbm, out_ref, g_ref, sem):
    copy = pltpu.make_async_copy(g_hbm, g_ref, sem)
    copy.start()
    copy.wait()
    cum = piece_sums(g_ref[1])
    own = g_ref[0] - cum
    for h in range(own.shape[0]):
        out_ref[h, 0:1, :] = own[h : h + 1]
        out_ref[h, 1:2, :] = cum[h : h + 1]


def gate_sums(gate_pre):
    kinds, heads, n = gate_pre.shape
    return pl.pallas_call(
        gate_kernel,
        in_specs=[HBM],
        out_specs=VMEM,
        out_shape=jax.ShapeDtypeStruct((heads, kinds, n), F32),
        scratch_shapes=[pltpu.VMEM(gate_pre.shape, F32), pltpu.SemaphoreType.DMA(())],
        compiler_params=pltpu.CompilerParams(vmem_limit_bytes=4 * MIB),
        name="gate_sums",
    )(in_hbm(gate_pre))


def turned_kernel(k_hbm, v_hbm, kt_ref, v_ref, k_ref, k_sem, v_sem):
    copies = []
    for j in range(BLOCKS):
        span = pl.ds(j * QB, QB)
        copies.append(pltpu.make_async_copy(k_hbm.at[span], k_ref.at[span], k_sem.at[j]))
        copies[-1].start()
    values = pltpu.make_async_copy(v_hbm, v_ref, v_sem)
    values.start()
    for j in range(BLOCKS):
        span = pl.ds(j * QB, QB)
        copies[j].wait()
        kt_ref[:, span] = k_ref[span, :].T
    values.wait()


def turned(keys, values):
    return pl.pallas_call(
        turned_kernel,
        in_specs=[HBM] * 2,
        out_specs=[VMEM] * 2,
        out_shape=[jax.ShapeDtypeStruct((DQK, TOKS), BF16), jax.ShapeDtypeStruct((TOKS, DV), BF16)],
        scratch_shapes=[
            pltpu.VMEM((TOKS, DQK), BF16),
            pltpu.SemaphoreType.DMA((BLOCKS,)),
            pltpu.SemaphoreType.DMA(()),
        ],
        compiler_params=pltpu.CompilerParams(vmem_limit_bytes=4 * MIB),
        cost_estimate=pl.CostEstimate(flops=0, bytes_accessed=4 * MIB, transcendentals=0),
        name="turn_keys",
    )(in_hbm(keys), in_hbm(values))


def state_kernel(g_ref, kt_ref, v_ref, own_ref, one_ref, two_ref, three_ref, tick_ref, w_ref, acc_ref):
    own = g_ref[:, 0, :]
    cum = g_ref[:, 1, :]
    later = jnp.broadcast_to(cum[:, PIECE - 1 :], cum.shape)
    row = lax.broadcasted_iota(jnp.int32, cum.shape, 0)
    for shift in (1, 2, 4):
        moved = pltpu.roll(later, PIECES - shift, 0)
        later = later + jnp.where(row + shift < PIECES, moved, 0.0)
    reach = own + later
    stab = jnp.max(jnp.max(reach, axis=1, keepdims=True), axis=0, keepdims=True)
    w_ref[...] = jnp.exp(reach - stab) * (DQK**-0.5)
    norm = jnp.zeros((24, DQK), F32)
    for j in range(BLOCKS):
        span = pl.ds(j * QB, QB)
        weight = jnp.concatenate([w_ref[2 * j : 2 * j + 1, :], w_ref[2 * j + 1 : 2 * j + 2, :]], axis=1)
        k = kt_ref[:, span]
        scaled = (k.astype(F32) * weight).astype(BF16)
        parts = [jnp.broadcast_to(p.astype(F32), (8, QB)) for p in three_parts(weight)]
        parts = jnp.concatenate(parts, axis=0).astype(BF16)
        norm += lax.dot_general(parts, k, (((1,), (1,)), ((), ())), preferred_element_type=F32)
        product = jnp.dot(scaled, v_ref[span, :], preferred_element_type=F32)
        if j:
            product += acc_ref[...].reshape(DQK, DV)
        acc_ref[...] = product.reshape(ZS, XS, ROWS, DV)
    norm = norm[0:8] + norm[8:16] + norm[16:24]
    norm = jnp.concatenate([norm[0:1, :LANES], norm[0:1, LANES:]], axis=0)
    extra = tail_of(norm, stab, later[0:1, :LANES])
    x = place_of("ctx_1")
    for k, ref in enumerate((own_ref, one_ref, two_ref, three_ref)):
        to = lax.rem(x + k, XS)
        for z in range(ZS):
            ref[:, z * DV : (z + 1) * DV] = acc_ref[z, pl.ds(to, 1)].reshape(ROWS, DV)
        ref[:, SLICE:] = extra
    tick_ref[...] = extra


def state(gates, keys_t, values):
    return pl.pallas_call(
        state_kernel,
        in_specs=[VMEM, VMEM, VMEM],
        out_specs=[VMEM] * 5,
        out_shape=[jax.ShapeDtypeStruct((ROWS, SENT), F32)] * 4 + [jax.ShapeDtypeStruct((8, LANES), F32)],
        scratch_shapes=[
            pltpu.VMEM((PIECES, PIECE), F32),
            pltpu.VMEM((ZS, XS, ROWS, DV), F32),
        ],
        compiler_params=pltpu.CompilerParams(vmem_limit_bytes=12 * MIB),
        cost_estimate=pl.CostEstimate(flops=600_000_000, bytes_accessed=5 * MIB, transcendentals=0),
        name="shard_state",
    )(gates, keys_t, values)


def tail_of(norm, stab, total):
    row = lax.broadcasted_iota(jnp.int32, (8, LANES), 0)
    tail = jnp.where(row == 0, norm[0:1], norm[1:2])
    return jnp.where(row == 2, stab, jnp.where(row == 3, total, tail))


def pieces_of(tail):
    return tail[0:2, :], tail[2:3, :], tail[3:4, :]


def chain_of(early, late):
    norm_e, stab_e, total_e = early
    norm_l, stab_l, total_l = late
    shifted = stab_e + total_l
    stab = jnp.maximum(shifted, stab_l)
    keep, take = jnp.exp(shifted - stab), jnp.exp(stab_l - stab)
    return keep, take, (keep * norm_e + take * norm_l, stab, total_e + total_l)


def spans():
    return [slice(z * DV, (z + 1) * DV) for z in range(ZS)]


def group_kernel(own_ref, one_ref, two_ref, three_ref, after_ref, out_ref, all_ref):
    x = place_of("ctx_1")
    for k, ref in enumerate((own_ref, one_ref, two_ref, three_ref)):
        at = lax.rem(x + XS - k, XS)
        all_ref[pl.ds(at, 1)] = ref[...].reshape(1, ROWS, SENT)
    small = pieces_of(all_ref[0, :, SLICE:])
    factors = []
    for j in range(1, XS):
        keep, take, small = chain_of(small, pieces_of(all_ref[j, :, SLICE:]))
        factors.append((wide(keep, DV), wide(take, DV)))
    for here in spans():
        memory = all_ref[0, :, here]
        for j, (keep, take) in enumerate(factors):
            memory = keep * memory + take * all_ref[j + 1, :, here]
        out_ref[:, here] = memory
    out_ref[:, SLICE:] = tail_of(*small)


def grouped(parts, after):
    return pl.pallas_call(
        group_kernel,
        in_specs=[VMEM] * 4 + [ANY],
        out_specs=[VMEM] * 2,
        out_shape=[
            jax.ShapeDtypeStruct((ROWS, SENT), F32),
            jax.ShapeDtypeStruct((XS, ROWS, SENT), F32),
        ],
        compiler_params=pltpu.CompilerParams(vmem_limit_bytes=4 * MIB),
        cost_estimate=pl.CostEstimate(flops=1_000_000, bytes_accessed=2 * MIB, transcendentals=0),
        name="group_states",
    )(*parts, after)


def merged(later, total_ref, got_ref):
    own, got = pieces_of(total_ref[:, SLICE:]), pieces_of(got_ref[:, SLICE:])
    first = [jnp.where(later, g, o) for g, o in zip(got, own)]
    second = [jnp.where(later, o, g) for g, o in zip(got, own)]
    keep, take, small = chain_of(first, second)
    return wide(jnp.where(later, take, keep), DV), wide(jnp.where(later, keep, take), DV), small


def brought(later, got_ref, before):
    bring, hold, small = chain_of(pieces_of(got_ref[:, SLICE:]), before)
    bring, hold = jnp.where(later, bring, 0.0), jnp.where(later, hold, 1.0)
    return wide(bring, DV), wide(hold, DV), [jnp.where(later, n, o) for n, o in zip(small, before)]


def later_of(z, bit):
    return lax.rem(lax.div(z, 1 << bit), 2) == 1


def first_round_kernel(total_ref, got_ref, after_ref, new_total, new_prefix):
    later = later_of(place_of("ctx_0"), 0)
    f_own, f_got, total = merged(later, total_ref, got_ref)
    nothing = (jnp.zeros((2, LANES), F32), jnp.full((1, LANES), NEG, F32), jnp.zeros((1, LANES), F32))
    bring, _, prefix = brought(later, got_ref, nothing)
    for here in spans():
        new_total[:, here] = f_own * total_ref[:, here] + f_got * got_ref[:, here]
        new_prefix[:, here] = bring * got_ref[:, here]
    new_total[:, SLICE:] = tail_of(*total)
    new_prefix[:, SLICE:] = tail_of(*prefix)


def next_round_kernel(total_ref, got_ref, prefix_ref, after_ref, new_total, new_prefix):
    later = later_of(place_of("ctx_0"), 1)
    f_own, f_got, total = merged(later, total_ref, got_ref)
    bring, hold, prefix = brought(later, got_ref, pieces_of(prefix_ref[:, SLICE:]))
    for here in spans():
        new_total[:, here] = f_own * total_ref[:, here] + f_got * got_ref[:, here]
        new_prefix[:, here] = bring * got_ref[:, here] + hold * prefix_ref[:, here]
    new_total[:, SLICE:] = tail_of(*total)
    new_prefix[:, SLICE:] = tail_of(*prefix)


def round_of(kernel, *args):
    return pl.pallas_call(
        kernel,
        in_specs=[VMEM] * (len(args) - 1) + [ANY],
        out_specs=[VMEM] * 2,
        out_shape=[jax.ShapeDtypeStruct((ROWS, SENT), F32)] * 2,
        compiler_params=pltpu.CompilerParams(vmem_limit_bytes=4 * MIB),
        cost_estimate=pl.CostEstimate(flops=1_000_000, bytes_accessed=MIB, transcendentals=0),
        name="merge_round",
    )(*args)


def spread_kernel(got_ref, prefix_ref, all_ref, after_ref, own_ref, one_ref, two_ref, three_ref, mine_ref, out_ref):
    x = place_of("ctx_1")
    later = later_of(place_of("ctx_0"), 2)
    bring, hold, small = brought(later, got_ref, pieces_of(prefix_ref[:, SLICE:]))
    mine = small
    factors = []
    for j in range(XS - 1):
        keep, take, small = chain_of(small, pieces_of(all_ref[j, :, SLICE:]))
        mine = [jnp.where(x == j + 1, n, o) for n, o in zip(small, mine)]
        factors.append((wide(keep, DV), wide(take, DV)))
    for here in spans():
        memory = bring * got_ref[:, here] + hold * prefix_ref[:, here]
        out_ref[0, :, here] = memory
        for j, (keep, take) in enumerate(factors):
            memory = keep * memory + take * all_ref[j, :, here]
            out_ref[j + 1, :, here] = memory
    for k, ref in enumerate((own_ref, one_ref, two_ref, three_ref)):
        ref[...] = out_ref[pl.ds(lax.rem(x + k, XS), 1)].reshape(ROWS, SLICE)
    mine_ref[...] = tail_of(*mine)


def spread(got, prefix, everything, after):
    return pl.pallas_call(
        spread_kernel,
        in_specs=[VMEM] * 3 + [ANY],
        out_specs=[VMEM] * 5,
        out_shape=[jax.ShapeDtypeStruct((ROWS, SLICE), F32)] * 4 + [jax.ShapeDtypeStruct((8, LANES), F32)],
        scratch_shapes=[pltpu.VMEM((XS, ROWS, SLICE), F32)],
        compiler_params=pltpu.CompilerParams(vmem_limit_bytes=4 * MIB),
        cost_estimate=pl.CostEstimate(flops=1_000_000, bytes_accessed=2 * MIB, transcendentals=0),
        name="spread_prefixes",
    )(got, prefix, everything, after)


def wide(x, n):
    return jnp.concatenate([x] * (n // LANES), axis=1)


def column(row):
    n = row.shape[1]
    return jnp.concatenate(
        [
            jnp.broadcast_to(row[:, at : at + LANES], (LANES, LANES)).T
            for at in range(0, n, LANES)
        ],
        axis=0,
    )


def tables(g_ref, table_ref):
    own, cum = [], []
    for r in range(0, PIECES, 2):
        first = g_ref[r, 1:2, :][:, PIECE - 1 :]
        own.append(jnp.concatenate([g_ref[r, 0:1, :], g_ref[r + 1, 0:1, :] - first], axis=1))
        cum.append(jnp.concatenate([g_ref[r, 1:2, :], g_ref[r + 1, 1:2, :] + first], axis=1))
    own = jnp.concatenate(own, axis=0)
    cum = jnp.concatenate(cum, axis=0)
    table_ref[0:BLOCKS, :] = own
    table_ref[BLOCKS : 2 * BLOCKS, :] = cum
    lane = lax.broadcasted_iota(jnp.int32, (BLOCKS, QB), 1)
    top = own
    shift = 1
    while shift < QB:
        moved = pltpu.roll(top, shift, 1)
        top = jnp.maximum(top, jnp.where(lane >= shift, moved, NEG))
        shift *= 2
    stab = jnp.full((1, 1), NEG, F32)
    for r in range(BLOCKS):
        at = 2 * BLOCKS + r
        table_ref[at : at + 1, :] = jnp.maximum(top[r : r + 1], stab)
        stab = jnp.maximum(stab, top[r : r + 1, QB - 1 :]) + cum[r : r + 1, QB - 1 :]


def local_kernel(blocks, table_ref, tick_ref, q_ref, k_ref, v_ref, num_ref, den_ref):
    for n, i in enumerate(blocks):
        here = pl.ds(n * QB, QB)
        top = column(table_ref[2 * BLOCKS + i : 2 * BLOCKS + i + 1, :])
        q = q_ref[pl.ds(i * QB, QB), :]

        def scores(j):
            at = pl.ds(pl.multiple_of(j * QB, QB), QB)
            return lax.dot_general(q, k_ref[at, :], (((1,), (1,)), ((), ())), preferred_element_type=F32)

        def sums(j, mixed):
            at = pl.ds(pl.multiple_of(j * QB, QB), QB)
            lanes = sum(mixed[:, c : c + LANES] for c in range(0, QB, LANES))
            return lanes, jnp.dot(mixed.astype(BF16), v_ref[at, :], preferred_element_type=F32)

        past = lax.broadcasted_iota(jnp.int32, (QB, QB), 0) >= lax.broadcasted_iota(jnp.int32, (QB, QB), 1)
        power = jnp.where(past, table_ref[i : i + 1, :] - wide(top, QB), NEG)
        den_ref[here, :], num_ref[here, :] = sums(i, jnp.exp(power) * scores(i))

        def earlier(m, shift):
            j = i - 1 - m
            shift = shift + table_ref[pl.ds(BLOCKS + j, 1), :][:, QB - 1 :]
            reach = table_ref[pl.ds(j, 1), :]
            peak = jnp.max(reach, axis=1, keepdims=True)
            lanes, product = sums(j, scores(j) * jnp.exp(reach - peak))
            factor = jnp.exp((peak + shift) - top)
            den_ref[here, :] += factor * lanes
            num_ref[here, :] += wide(factor, DV) * product
            return shift

        if i:
            lax.fori_loop(0, i, earlier, jnp.zeros((1, 1), F32))


def first_kernel(blocks, g_ref, tick_ref, q_hbm, k_hbm, v_ref, num_ref, den_ref, table_ref, q_ref, k_ref, q_sem, k_sem):
    copies = [pltpu.make_async_copy(q_hbm, q_ref, q_sem), pltpu.make_async_copy(k_hbm, k_ref, k_sem)]
    for copy in copies:
        copy.start()
    tables(g_ref, table_ref)
    for copy in copies:
        copy.wait()
    local_kernel(blocks, table_ref, tick_ref, q_ref, k_ref, v_ref, num_ref, den_ref)


def local(blocks, gates, tick, queries, keys, values, table=None):
    count = len(blocks)
    units = sum(blocks) + count
    first = table is None
    out_shape = [
        jax.ShapeDtypeStruct((count * QB, DV), F32),
        jax.ShapeDtypeStruct((count * QB, LANES), F32),
        jax.ShapeDtypeStruct((3 * BLOCKS, QB), F32),
        jax.ShapeDtypeStruct((TOKS, DQK), BF16),
        jax.ShapeDtypeStruct((TOKS, DQK), BF16),
    ][: 5 if first else 2]
    return pl.pallas_call(
        functools.partial(first_kernel if first else local_kernel, blocks),
        in_specs=[VMEM, ANY, HBM, HBM, VMEM] if first else [VMEM, ANY] + [VMEM] * 3,
        out_specs=[VMEM] * len(out_shape),
        out_shape=out_shape,
        scratch_shapes=[pltpu.SemaphoreType.DMA(())] * (2 * first),
        compiler_params=pltpu.CompilerParams(vmem_limit_bytes=8 * MIB),
        cost_estimate=pl.CostEstimate(flops=800_000_000 * units, bytes_accessed=MIB * units, transcendentals=0),
        name="within_shard",
    )(*((gates, tick, in_hbm(queries), in_hbm(keys), values) if first else (table, tick, queries, keys, values)))


def scale_kernel(table_ref, mine_ref, q_ref, total_ref, got_ref, *refs):
    dens, (kept_ref, carried_ref, close_ref, norm_ref, top_ref) = refs[:-5], refs[-5:]
    z = place_of("ctx_0")
    here = pl.ds(pl.multiple_of(z * DV, DV), DV)
    f_own, f_got, (end_norm, end_top, _) = merged(later_of(z, 2), total_ref, got_ref)
    close_ref[0] = f_own * total_ref[:, here] + f_got * got_ref[:, here]
    norm_ref[:, :LANES] = end_norm[0:1]
    norm_ref[:, LANES:] = end_norm[1:2]
    top_ref[...] = end_top
    norm, log_in, _ = pieces_of(mine_ref)
    norm = jnp.concatenate([norm[0:1], norm[1:2]], axis=1)
    place = {i: (dens[n], m) for n, blocks in enumerate(PARTS) for m, i in enumerate(blocks)}
    for i in range(BLOCKS):
        den_ref, m = place[i]
        here, there = pl.ds(i * QB, QB), pl.ds(m * QB, QB)
        top = column(table_ref[2 * BLOCKS + i : 2 * BLOCKS + i + 1, :])
        peak = jnp.maximum(top, log_in)
        kept, carried = jnp.exp(top - peak) * (DQK**-0.5), jnp.exp(log_in - peak)
        from_norm = jnp.sum(q_ref[here, :].astype(F32) * norm, axis=1, keepdims=True)
        denom = jnp.sum(den_ref[there, :], axis=1, keepdims=True) * kept + carried * from_norm
        inverse = 1.0 / jnp.maximum(jnp.abs(denom), 1.0)
        kept_ref[here, :] = kept * inverse
        carried_ref[here, :] = carried * inverse
        log_in = log_in + table_ref[BLOCKS + i : BLOCKS + i + 1, :][:, QB - 1 :]


def scales(table, mine, queries, total, got, dens):
    return pl.pallas_call(
        scale_kernel,
        in_specs=[VMEM] * (5 + len(dens)),
        out_specs=[VMEM] * 5,
        out_shape=[jax.ShapeDtypeStruct((TOKS, LANES), F32)] * 2
        + [
            jax.ShapeDtypeStruct((1, ROWS, DV), F32),
            jax.ShapeDtypeStruct((1, DQK), F32),
            jax.ShapeDtypeStruct((1, LANES), F32),
        ],
        compiler_params=pltpu.CompilerParams(vmem_limit_bytes=4 * MIB),
        cost_estimate=pl.CostEstimate(flops=600_000_000, bytes_accessed=4 * MIB, transcendentals=0),
        name="row_scales",
    )(table, mine, queries, total, got, *dens)


def joined_kernel(q_ref, own_ref, one_ref, two_ref, three_ref, kept_ref, carried_ref, *refs):
    nums, (out_hbm, mem_ref, mem_b_ref, out_ref, sem) = refs[:-5], refs[-5:]
    x = place_of("ctx_1")
    for k, ref in enumerate((own_ref, one_ref, two_ref, three_ref)):
        at = lax.rem(x + XS - k, XS)
        for z, here in enumerate(spans()):
            mem_ref[z, pl.ds(at, 1)] = ref[:, here].reshape(1, ROWS, DV)
    mem_b_ref[...] = mem_ref[...].reshape(DQK, DV).astype(BF16)
    copies = []
    for n, blocks in enumerate(PARTS):
        for m, i in enumerate(blocks):
            for half in range(0, QB, PIECE):
                span, there = pl.ds(i * QB + half, PIECE), pl.ds(m * QB + half, PIECE)
                product = jnp.dot(q_ref[span, :], mem_b_ref[...], preferred_element_type=F32)
                local_part = wide(kept_ref[span, :], DV) * nums[n][there, :]
                out_ref[span, :] = (local_part + wide(carried_ref[span, :], DV) * product).astype(BF16)
                copies.append(pltpu.make_async_copy(out_ref.at[span], out_hbm.at[span], sem.at[len(copies)]))
                copies[-1].start()
    for copy in copies:
        copy.wait()


def joined(queries, parts, kept, carried, nums):
    return pl.pallas_call(
        joined_kernel,
        in_specs=[VMEM] * (7 + len(nums)),
        out_specs=HBM,
        out_shape=jax.ShapeDtypeStruct((TOKS, DV), BF16),
        scratch_shapes=[
            pltpu.VMEM((ZS, XS, ROWS, DV), F32),
            pltpu.VMEM((DQK, DV), BF16),
            pltpu.VMEM((TOKS, DV), BF16),
            pltpu.SemaphoreType.DMA((PIECES,)),
        ],
        compiler_params=pltpu.CompilerParams(vmem_limit_bytes=8 * MIB),
        cost_estimate=pl.CostEstimate(flops=600_000_000, bytes_accessed=9 * MIB, transcendentals=0),
        name="join_memory",
    )(queries, *parts, kept, carried, *nums)


def exchanged(x, axis):
    return lax.all_to_all(x, axis, split_axis=0, concat_axis=0, tiled=True)


def around(parts):
    moved = [parts[0]]
    for k in range(1, XS):
        moved.append(lax.ppermute(parts[k], "ctx_1", [(i, (i + k) % XS) for i in range(XS)]))
    return moved


def swapped(x, partner):
    return lax.ppermute(x, "ctx_0", [(i, partner(i)) for i in range(ZS)])


def on_device(queries, keys, values, gate_pre):
    gates = exchanged(gate_sums(gate_pre), "head")
    keys_t, values = turned(keys, values)
    *parts, tick = state(gates, keys_t, values)
    moved = around(parts)
    num_a, den_a, table, queries, keys = local(PARTS[0], gates, tick, queries, keys, values)
    qkv = (queries, keys, values)
    total, everything = grouped(moved, den_a)
    got = swapped(total, lambda i: i ^ 1)
    total, prefix = round_of(first_round_kernel, total, got, den_a)
    got = swapped(total, lambda i: i ^ 2)
    num_b, den_b = local(PARTS[1], None, prefix, *qkv, table)
    total, prefix = round_of(next_round_kernel, total, got, prefix, den_b)
    got = swapped(total, lambda i: (6, 7, 5, 4, 3, 2, 0, 1)[i])
    num_c, den_c = local(PARTS[2], None, prefix, *qkv, table)
    *parts, mine = spread(got, prefix, everything, den_c)
    moved = around(parts)
    kept, carried, closing, final_norm, top = scales(table, mine, queries, total, got, [den_a, den_b, den_c])
    hidden = joined(queries, moved, kept, carried, [num_a, num_b, num_c])
    return (hidden, closing, final_norm, top[0, :1])


def solution(mesh):
    split = Mesh(mesh.devices.reshape(8, 4, mesh.shape["head"]), ("ctx_0", "ctx_1", "head"))
    in_specs = (P(CTX, "head"), P(CTX, "head"), P(CTX, "head"), P(None, None, CTX_HEAD))
    out_specs = (P(CTX, "head"), P("head", CTX, None), P("head", None), P("head"))
    return jax.shard_map(
        on_device, mesh=split, in_specs=in_specs, out_specs=out_specs, check_vma=False
    )
```

```python
import functools

import jax
import jax.numpy as jnp
from jax import lax
from jax.experimental import pallas as pl
from jax.experimental.pallas import tpu as pltpu
from jax.sharding import Mesh
from jax.sharding import PartitionSpec as P

DQK = 256
DV = 512
XS = 4
ZS = 8
ROWS = DQK // (XS * ZS)
PIECES = 8
PIECE = 256
LANES = 128
SLICE = ZS * DV
SENT = SLICE + LANES
TOKS = PIECES * PIECE
QB = 512
BLOCKS = TOKS // QB
PARTS = ((3,), (0, 1), (2,))
CTX = ("ctx_0", "ctx_1")
CTX_HEAD = ("ctx_0", "ctx_1", "head")
NEG = -1e30
F32 = jnp.float32
BF16 = jnp.bfloat16
VMEM = pl.BlockSpec(memory_space=pltpu.VMEM)
HBM = pl.BlockSpec(memory_space=pltpu.HBM)
ANY = pl.BlockSpec(memory_space=pl.ANY)
MIB = 1 << 20


def in_hbm(x):
    return pltpu.with_memory_space_constraint(x, pltpu.HBM)


def place_of(axis):
    return lax.axis_index(axis).astype(jnp.int32)


def log_sigmoid(x):
    z = jnp.exp(-jnp.abs(x))
    s = z / (2.0 + z)
    s2 = s * s
    tail = jnp.full_like(s, 1.0 / 17.0)
    for n in (15, 13, 11, 9, 7, 5, 3, 1):
        tail = tail * s2 + 1.0 / n
    return jnp.minimum(x, 0.0) - 2.0 * s * tail


def three_parts(x):
    high = x.astype(BF16)
    rest = x - high.astype(F32)
    mid = rest.astype(BF16)
    low = (rest - mid.astype(F32)).astype(BF16)
    return high, mid, low


def piece_sums(forget):
    n = forget.shape[1]
    upto = lax.broadcasted_iota(jnp.int32, (n, n), 0) <= lax.broadcasted_iota(jnp.int32, (n, n), 1)
    ones = jnp.where(upto, 1.0, 0.0).astype(BF16)
    parts = jnp.concatenate([p.astype(F32) for p in three_parts(log_sigmoid(forget))], axis=0)
    sums = jnp.dot(parts.astype(BF16), ones, preferred_element_type=F32)
    k = forget.shape[0]
    return sums[:k] + sums[k : 2 * k] + sums[2 * k :]


def gate_kernel(g_hbm, out_ref, g_ref, sem):
    copy = pltpu.make_async_copy(g_hbm, g_ref, sem)
    copy.start()
    copy.wait()
    cum = piece_sums(g_ref[1])
    own = g_ref[0] - cum
    for h in range(own.shape[0]):
        out_ref[h, 0:1, :] = own[h : h + 1]
        out_ref[h, 1:2, :] = cum[h : h + 1]


def gate_sums(gate_pre):
    kinds, heads, n = gate_pre.shape
    return pl.pallas_call(
        gate_kernel,
        in_specs=[HBM],
        out_specs=VMEM,
        out_shape=jax.ShapeDtypeStruct((heads, kinds, n), F32),
        scratch_shapes=[pltpu.VMEM(gate_pre.shape, F32), pltpu.SemaphoreType.DMA(())],
        compiler_params=pltpu.CompilerParams(vmem_limit_bytes=4 * MIB),
        name="gate_sums",
    )(in_hbm(gate_pre))


def turned_kernel(k_hbm, v_hbm, kt_ref, v_ref, k_ref, k_sem, v_sem):
    copies = []
    for j in range(BLOCKS):
        span = pl.ds(j * QB, QB)
        copies.append(pltpu.make_async_copy(k_hbm.at[span], k_ref.at[span], k_sem.at[j]))
        copies[-1].start()
    values = pltpu.make_async_copy(v_hbm, v_ref, v_sem)
    values.start()
    for j in range(BLOCKS):
        span = pl.ds(j * QB, QB)
        copies[j].wait()
        kt_ref[:, span] = k_ref[span, :].T
    values.wait()


def turned(keys, values):
    return pl.pallas_call(
        turned_kernel,
        in_specs=[HBM] * 2,
        out_specs=[VMEM] * 2,
        out_shape=[jax.ShapeDtypeStruct((DQK, TOKS), BF16), jax.ShapeDtypeStruct((TOKS, DV), BF16)],
        scratch_shapes=[
            pltpu.VMEM((TOKS, DQK), BF16),
            pltpu.SemaphoreType.DMA((BLOCKS,)),
            pltpu.SemaphoreType.DMA(()),
        ],
        compiler_params=pltpu.CompilerParams(vmem_limit_bytes=4 * MIB),
        cost_estimate=pl.CostEstimate(flops=0, bytes_accessed=4 * MIB, transcendentals=0),
        name="turn_keys",
    )(in_hbm(keys), in_hbm(values))


def state_kernel(g_ref, kt_ref, v_ref, own_ref, one_ref, two_ref, three_ref, tick_ref, w_ref, acc_ref):
    own = g_ref[:, 0, :]
    cum = g_ref[:, 1, :]
    later = jnp.broadcast_to(cum[:, PIECE - 1 :], cum.shape)
    row = lax.broadcasted_iota(jnp.int32, cum.shape, 0)
    for shift in (1, 2, 4):
        moved = pltpu.roll(later, PIECES - shift, 0)
        later = later + jnp.where(row + shift < PIECES, moved, 0.0)
    reach = own + later
    stab = jnp.max(jnp.max(reach, axis=1, keepdims=True), axis=0, keepdims=True)
    w_ref[...] = jnp.exp(reach - stab) * (DQK**-0.5)
    norm = jnp.zeros((24, DQK), F32)
    for j in range(BLOCKS):
        span = pl.ds(j * QB, QB)
        weight = jnp.concatenate([w_ref[2 * j : 2 * j + 1, :], w_ref[2 * j + 1 : 2 * j + 2, :]], axis=1)
        k = kt_ref[:, span]
        scaled = (k.astype(F32) * weight).astype(BF16)
        parts = [jnp.broadcast_to(p.astype(F32), (8, QB)) for p in three_parts(weight)]
        parts = jnp.concatenate(parts, axis=0).astype(BF16)
        norm += lax.dot_general(parts, k, (((1,), (1,)), ((), ())), preferred_element_type=F32)
        product = jnp.dot(scaled, v_ref[span, :], preferred_element_type=F32)
        if j:
            product += acc_ref[...].reshape(DQK, DV)
        acc_ref[...] = product.reshape(ZS, XS, ROWS, DV)
    norm = norm[0:8] + norm[8:16] + norm[16:24]
    norm = jnp.concatenate([norm[0:1, :LANES], norm[0:1, LANES:]], axis=0)
    extra = tail_of(norm, stab, later[0:1, :LANES])
    x = place_of("ctx_1")
    for k, ref in enumerate((own_ref, one_ref, two_ref, three_ref)):
        to = lax.rem(x + k, XS)
        for z in range(ZS):
            ref[:, z * DV : (z + 1) * DV] = acc_ref[z, pl.ds(to, 1)].reshape(ROWS, DV)
        ref[:, SLICE:] = extra
    tick_ref[...] = extra


def state(gates, keys_t, values):
    return pl.pallas_call(
        state_kernel,
        in_specs=[VMEM, VMEM, VMEM],
        out_specs=[VMEM] * 5,
        out_shape=[jax.ShapeDtypeStruct((ROWS, SENT), F32)] * 4 + [jax.ShapeDtypeStruct((8, LANES), F32)],
        scratch_shapes=[
            pltpu.VMEM((PIECES, PIECE), F32),
            pltpu.VMEM((ZS, XS, ROWS, DV), F32),
        ],
        compiler_params=pltpu.CompilerParams(vmem_limit_bytes=12 * MIB),
        cost_estimate=pl.CostEstimate(flops=600_000_000, bytes_accessed=5 * MIB, transcendentals=0),
        name="shard_state",
    )(gates, keys_t, values)


def tail_of(norm, stab, total):
    row = lax.broadcasted_iota(jnp.int32, (8, LANES), 0)
    tail = jnp.where(row == 0, norm[0:1], norm[1:2])
    return jnp.where(row == 2, stab, jnp.where(row == 3, total, tail))


def pieces_of(tail):
    return tail[0:2, :], tail[2:3, :], tail[3:4, :]


def chain_of(early, late):
    norm_e, stab_e, total_e = early
    norm_l, stab_l, total_l = late
    shifted = stab_e + total_l
    stab = jnp.maximum(shifted, stab_l)
    keep, take = jnp.exp(shifted - stab), jnp.exp(stab_l - stab)
    return keep, take, (keep * norm_e + take * norm_l, stab, total_e + total_l)


def spans():
    return [slice(z * DV, (z + 1) * DV) for z in range(ZS)]


def group_kernel(own_ref, one_ref, two_ref, three_ref, after_ref, out_ref, all_ref):
    x = place_of("ctx_1")
    for k, ref in enumerate((own_ref, one_ref, two_ref, three_ref)):
        at = lax.rem(x + XS - k, XS)
        all_ref[pl.ds(at, 1)] = ref[...].reshape(1, ROWS, SENT)
    small = pieces_of(all_ref[0, :, SLICE:])
    factors = []
    for j in range(1, XS):
        keep, take, small = chain_of(small, pieces_of(all_ref[j, :, SLICE:]))
        factors.append((wide(keep, DV), wide(take, DV)))
    for here in spans():
        memory = all_ref[0, :, here]
        for j, (keep, take) in enumerate(factors):
            memory = keep * memory + take * all_ref[j + 1, :, here]
        out_ref[:, here] = memory
    out_ref[:, SLICE:] = tail_of(*small)


def grouped(parts, after):
    return pl.pallas_call(
        group_kernel,
        in_specs=[VMEM] * 4 + [ANY],
        out_specs=[VMEM] * 2,
        out_shape=[
            jax.ShapeDtypeStruct((ROWS, SENT), F32),
            jax.ShapeDtypeStruct((XS, ROWS, SENT), F32),
        ],
        compiler_params=pltpu.CompilerParams(vmem_limit_bytes=4 * MIB),
        cost_estimate=pl.CostEstimate(flops=1_000_000, bytes_accessed=2 * MIB, transcendentals=0),
        name="group_states",
    )(*parts, after)


def merged(later, total_ref, got_ref):
    own, got = pieces_of(total_ref[:, SLICE:]), pieces_of(got_ref[:, SLICE:])
    first = [jnp.where(later, g, o) for g, o in zip(got, own)]
    second = [jnp.where(later, o, g) for g, o in zip(got, own)]
    keep, take, small = chain_of(first, second)
    return wide(jnp.where(later, take, keep), DV), wide(jnp.where(later, keep, take), DV), small


def brought(later, got_ref, before):
    bring, hold, small = chain_of(pieces_of(got_ref[:, SLICE:]), before)
    bring, hold = jnp.where(later, bring, 0.0), jnp.where(later, hold, 1.0)
    return wide(bring, DV), wide(hold, DV), [jnp.where(later, n, o) for n, o in zip(small, before)]


def later_of(z, bit):
    return lax.rem(lax.div(z, 1 << bit), 2) == 1


def first_round_kernel(total_ref, got_ref, after_ref, new_total, new_prefix):
    later = later_of(place_of("ctx_0"), 0)
    f_own, f_got, total = merged(later, total_ref, got_ref)
    nothing = (jnp.zeros((2, LANES), F32), jnp.full((1, LANES), NEG, F32), jnp.zeros((1, LANES), F32))
    bring, _, prefix = brought(later, got_ref, nothing)
    for here in spans():
        new_total[:, here] = f_own * total_ref[:, here] + f_got * got_ref[:, here]
        new_prefix[:, here] = bring * got_ref[:, here]
    new_total[:, SLICE:] = tail_of(*total)
    new_prefix[:, SLICE:] = tail_of(*prefix)


def next_round_kernel(total_ref, got_ref, prefix_ref, after_ref, new_total, new_prefix):
    later = later_of(place_of("ctx_0"), 1)
    f_own, f_got, total = merged(later, total_ref, got_ref)
    bring, hold, prefix = brought(later, got_ref, pieces_of(prefix_ref[:, SLICE:]))
    for here in spans():
        new_total[:, here] = f_own * total_ref[:, here] + f_got * got_ref[:, here]
        new_prefix[:, here] = bring * got_ref[:, here] + hold * prefix_ref[:, here]
    new_total[:, SLICE:] = tail_of(*total)
    new_prefix[:, SLICE:] = tail_of(*prefix)


def round_of(kernel, *args):
    return pl.pallas_call(
        kernel,
        in_specs=[VMEM] * (len(args) - 1) + [ANY],
        out_specs=[VMEM] * 2,
        out_shape=[jax.ShapeDtypeStruct((ROWS, SENT), F32)] * 2,
        compiler_params=pltpu.CompilerParams(vmem_limit_bytes=4 * MIB),
        cost_estimate=pl.CostEstimate(flops=1_000_000, bytes_accessed=MIB, transcendentals=0),
        name="merge_round",
    )(*args)


def spread_kernel(got_ref, prefix_ref, all_ref, after_ref, own_ref, one_ref, two_ref, three_ref, mine_ref, out_ref):
    x = place_of("ctx_1")
    later = later_of(place_of("ctx_0"), 2)
    bring, hold, small = brought(later, got_ref, pieces_of(prefix_ref[:, SLICE:]))
    mine = small
    factors = []
    for j in range(XS - 1):
        keep, take, small = chain_of(small, pieces_of(all_ref[j, :, SLICE:]))
        mine = [jnp.where(x == j + 1, n, o) for n, o in zip(small, mine)]
        factors.append((wide(keep, DV), wide(take, DV)))
    for z, here in enumerate(spans()):
        memory = bring * got_ref[:, here] + hold * prefix_ref[:, here]
        out_ref[0, z] = memory
        for j, (keep, take) in enumerate(factors):
            memory = keep * memory + take * all_ref[j, :, here]
            out_ref[j + 1, z] = memory
    for k, ref in enumerate((own_ref, one_ref, two_ref, three_ref)):
        ref[...] = out_ref[pl.ds(lax.rem(x + k, XS), 1)].reshape(ZS, ROWS, DV)
    mine_ref[...] = tail_of(*mine)


def spread(got, prefix, everything, after):
    return pl.pallas_call(
        spread_kernel,
        in_specs=[VMEM] * 3 + [ANY],
        out_specs=[VMEM] * 5,
        out_shape=[jax.ShapeDtypeStruct((ZS, ROWS, DV), F32)] * 4 + [jax.ShapeDtypeStruct((8, LANES), F32)],
        scratch_shapes=[pltpu.VMEM((XS, ZS, ROWS, DV), F32)],
        compiler_params=pltpu.CompilerParams(vmem_limit_bytes=4 * MIB),
        cost_estimate=pl.CostEstimate(flops=1_000_000, bytes_accessed=2 * MIB, transcendentals=0),
        name="spread_prefixes",
    )(got, prefix, everything, after)


def wide(x, n):
    return jnp.concatenate([x] * (n // LANES), axis=1)


def column(row):
    n = row.shape[1]
    return jnp.concatenate(
        [
            jnp.broadcast_to(row[:, at : at + LANES], (LANES, LANES)).T
            for at in range(0, n, LANES)
        ],
        axis=0,
    )


def tables(g_ref, table_ref):
    own, cum = [], []
    for r in range(0, PIECES, 2):
        first = g_ref[r, 1:2, :][:, PIECE - 1 :]
        own.append(jnp.concatenate([g_ref[r, 0:1, :], g_ref[r + 1, 0:1, :] - first], axis=1))
        cum.append(jnp.concatenate([g_ref[r, 1:2, :], g_ref[r + 1, 1:2, :] + first], axis=1))
    own = jnp.concatenate(own, axis=0)
    cum = jnp.concatenate(cum, axis=0)
    table_ref[0:BLOCKS, :] = own
    table_ref[BLOCKS : 2 * BLOCKS, :] = cum
    lane = lax.broadcasted_iota(jnp.int32, (BLOCKS, QB), 1)
    top = own
    shift = 1
    while shift < QB:
        moved = pltpu.roll(top, shift, 1)
        top = jnp.maximum(top, jnp.where(lane >= shift, moved, NEG))
        shift *= 2
    stab = jnp.full((1, 1), NEG, F32)
    for r in range(BLOCKS):
        at = 2 * BLOCKS + r
        table_ref[at : at + 1, :] = jnp.maximum(top[r : r + 1], stab)
        stab = jnp.maximum(stab, top[r : r + 1, QB - 1 :]) + cum[r : r + 1, QB - 1 :]


def local_kernel(blocks, table_ref, tick_ref, q_ref, k_ref, v_ref, num_ref, den_ref):
    for n, i in enumerate(blocks):
        here = pl.ds(n * QB, QB)
        top = column(table_ref[2 * BLOCKS + i : 2 * BLOCKS + i + 1, :])
        q = q_ref[pl.ds(i * QB, QB), :]

        def scores(j):
            at = pl.ds(pl.multiple_of(j * QB, QB), QB)
            return lax.dot_general(q, k_ref[at, :], (((1,), (1,)), ((), ())), preferred_element_type=F32)

        def sums(j, mixed):
            at = pl.ds(pl.multiple_of(j * QB, QB), QB)
            lanes = sum(mixed[:, c : c + LANES] for c in range(0, QB, LANES))
            return lanes, jnp.dot(mixed.astype(BF16), v_ref[at, :], preferred_element_type=F32)

        past = lax.broadcasted_iota(jnp.int32, (QB, QB), 0) >= lax.broadcasted_iota(jnp.int32, (QB, QB), 1)
        power = jnp.where(past, table_ref[i : i + 1, :] - wide(top, QB), NEG)
        den_ref[here, :], num_ref[here, :] = sums(i, jnp.exp(power) * scores(i))

        def earlier(m, shift):
            j = i - 1 - m
            shift = shift + table_ref[pl.ds(BLOCKS + j, 1), :][:, QB - 1 :]
            reach = table_ref[pl.ds(j, 1), :]
            peak = jnp.max(reach, axis=1, keepdims=True)
            lanes, product = sums(j, scores(j) * jnp.exp(reach - peak))
            factor = jnp.exp((peak + shift) - top)
            den_ref[here, :] += factor * lanes
            num_ref[here, :] += wide(factor, DV) * product
            return shift

        if i:
            lax.fori_loop(0, i, earlier, jnp.zeros((1, 1), F32))


def first_kernel(blocks, g_ref, tick_ref, q_hbm, k_hbm, v_ref, num_ref, den_ref, table_ref, q_ref, k_ref, q_sem, k_sem):
    copies = [pltpu.make_async_copy(q_hbm, q_ref, q_sem), pltpu.make_async_copy(k_hbm, k_ref, k_sem)]
    for copy in copies:
        copy.start()
    tables(g_ref, table_ref)
    for copy in copies:
        copy.wait()
    local_kernel(blocks, table_ref, tick_ref, q_ref, k_ref, v_ref, num_ref, den_ref)


def local(blocks, gates, tick, queries, keys, values, table=None):
    count = len(blocks)
    units = sum(blocks) + count
    first = table is None
    out_shape = [
        jax.ShapeDtypeStruct((count * QB, DV), F32),
        jax.ShapeDtypeStruct((count * QB, LANES), F32),
        jax.ShapeDtypeStruct((3 * BLOCKS, QB), F32),
        jax.ShapeDtypeStruct((TOKS, DQK), BF16),
        jax.ShapeDtypeStruct((TOKS, DQK), BF16),
    ][: 5 if first else 2]
    return pl.pallas_call(
        functools.partial(first_kernel if first else local_kernel, blocks),
        in_specs=[VMEM, ANY, HBM, HBM, VMEM] if first else [VMEM, ANY] + [VMEM] * 3,
        out_specs=[VMEM] * len(out_shape),
        out_shape=out_shape,
        scratch_shapes=[pltpu.SemaphoreType.DMA(())] * (2 * first),
        compiler_params=pltpu.CompilerParams(vmem_limit_bytes=8 * MIB),
        cost_estimate=pl.CostEstimate(flops=800_000_000 * units, bytes_accessed=MIB * units, transcendentals=0),
        name="within_shard",
    )(*((gates, tick, in_hbm(queries), in_hbm(keys), values) if first else (table, tick, queries, keys, values)))


def scale_kernel(table_ref, mine_ref, q_ref, total_ref, got_ref, *refs):
    dens, (kept_ref, carried_ref, close_ref, norm_ref, top_ref) = refs[:-5], refs[-5:]
    z = place_of("ctx_0")
    here = pl.ds(pl.multiple_of(z * DV, DV), DV)
    f_own, f_got, (end_norm, end_top, _) = merged(later_of(z, 2), total_ref, got_ref)
    close_ref[0] = f_own * total_ref[:, here] + f_got * got_ref[:, here]
    norm_ref[:, :LANES] = end_norm[0:1]
    norm_ref[:, LANES:] = end_norm[1:2]
    top_ref[...] = end_top
    norm, log_in, _ = pieces_of(mine_ref)
    norm = jnp.concatenate([norm[0:1], norm[1:2]], axis=1)
    place = {i: (dens[n], m) for n, blocks in enumerate(PARTS) for m, i in enumerate(blocks)}
    for i in range(BLOCKS):
        den_ref, m = place[i]
        here, there = pl.ds(i * QB, QB), pl.ds(m * QB, QB)
        top = column(table_ref[2 * BLOCKS + i : 2 * BLOCKS + i + 1, :])
        peak = jnp.maximum(top, log_in)
        kept, carried = jnp.exp(top - peak) * (DQK**-0.5), jnp.exp(log_in - peak)
        from_norm = jnp.sum(q_ref[here, :].astype(F32) * norm, axis=1, keepdims=True)
        denom = jnp.sum(den_ref[there, :], axis=1, keepdims=True) * kept + carried * from_norm
        inverse = 1.0 / jnp.maximum(jnp.abs(denom), 1.0)
        kept_ref[here, :] = kept * inverse
        carried_ref[here, :] = carried * inverse
        log_in = log_in + table_ref[BLOCKS + i : BLOCKS + i + 1, :][:, QB - 1 :]


def scales(table, mine, queries, total, got, dens):
    return pl.pallas_call(
        scale_kernel,
        in_specs=[VMEM] * (5 + len(dens)),
        out_specs=[VMEM] * 5,
        out_shape=[jax.ShapeDtypeStruct((TOKS, LANES), F32)] * 2
        + [
            jax.ShapeDtypeStruct((1, ROWS, DV), F32),
            jax.ShapeDtypeStruct((1, DQK), F32),
            jax.ShapeDtypeStruct((1, LANES), F32),
        ],
        compiler_params=pltpu.CompilerParams(vmem_limit_bytes=4 * MIB),
        cost_estimate=pl.CostEstimate(flops=600_000_000, bytes_accessed=4 * MIB, transcendentals=0),
        name="row_scales",
    )(table, mine, queries, total, got, *dens)


def joined_kernel(q_ref, own_ref, one_ref, two_ref, three_ref, kept_ref, carried_ref, *refs):
    nums, (out_hbm, mem_ref, mem_b_ref, out_ref, sem) = refs[:-5], refs[-5:]
    x = place_of("ctx_1")
    for k, ref in enumerate((own_ref, one_ref, two_ref, three_ref)):
        at = lax.rem(x + XS - k, XS)
        mem_ref[:, pl.ds(at, 1)] = ref[...].reshape(ZS, 1, ROWS, DV)
    mem_b_ref[...] = mem_ref[...].reshape(DQK, DV).astype(BF16)
    copies = []
    for n, blocks in enumerate(PARTS):
        for m, i in enumerate(blocks):
            for half in range(0, QB, PIECE):
                span, there = pl.ds(i * QB + half, PIECE), pl.ds(m * QB + half, PIECE)
                product = jnp.dot(q_ref[span, :], mem_b_ref[...], preferred_element_type=F32)
                local_part = wide(kept_ref[span, :], DV) * nums[n][there, :]
                out_ref[span, :] = (local_part + wide(carried_ref[span, :], DV) * product).astype(BF16)
                copies.append(pltpu.make_async_copy(out_ref.at[span], out_hbm.at[span], sem.at[len(copies)]))
                copies[-1].start()
    for copy in copies:
        copy.wait()


def joined(queries, parts, kept, carried, nums):
    return pl.pallas_call(
        joined_kernel,
        in_specs=[VMEM] * (7 + len(nums)),
        out_specs=HBM,
        out_shape=jax.ShapeDtypeStruct((TOKS, DV), BF16),
        scratch_shapes=[
            pltpu.VMEM((ZS, XS, ROWS, DV), F32),
            pltpu.VMEM((DQK, DV), BF16),
            pltpu.VMEM((TOKS, DV), BF16),
            pltpu.SemaphoreType.DMA((PIECES,)),
        ],
        compiler_params=pltpu.CompilerParams(vmem_limit_bytes=8 * MIB),
        cost_estimate=pl.CostEstimate(flops=600_000_000, bytes_accessed=9 * MIB, transcendentals=0),
        name="join_memory",
    )(queries, *parts, kept, carried, *nums)


def exchanged(x, axis):
    return lax.all_to_all(x, axis, split_axis=0, concat_axis=0, tiled=True)


def around(parts):
    moved = [parts[0]]
    for k in range(1, XS):
        moved.append(lax.ppermute(parts[k], "ctx_1", [(i, (i + k) % XS) for i in range(XS)]))
    return moved


def swapped(x, partner):
    return lax.ppermute(x, "ctx_0", [(i, partner(i)) for i in range(ZS)])


def on_device(queries, keys, values, gate_pre):
    gates = exchanged(gate_sums(gate_pre), "head")
    keys_t, values = turned(keys, values)
    *parts, tick = state(gates, keys_t, values)
    moved = around(parts)
    num_a, den_a, table, queries, keys = local(PARTS[0], gates, tick, queries, keys, values)
    qkv = (queries, keys, values)
    total, everything = grouped(moved, den_a)
    got = swapped(total, lambda i: i ^ 1)
    total, prefix = round_of(first_round_kernel, total, got, den_a)
    got = swapped(total, lambda i: i ^ 3)
    num_b, den_b = local(PARTS[1], None, prefix, *qkv, table)
    total, prefix = round_of(next_round_kernel, total, got, prefix, den_b)
    got = swapped(total, lambda i: (6, 7, 5, 4, 3, 2, 0, 1)[i])
    num_c, den_c = local(PARTS[2], None, prefix, *qkv, table)
    *parts, mine = spread(got, prefix, everything, den_c)
    moved = around(parts)
    kept, carried, closing, final_norm, top = scales(table, mine, queries, total, got, [den_a, den_b, den_c])
    hidden = joined(queries, moved, kept, carried, [num_a, num_b, num_c])
    return (hidden, closing, final_norm, top[0, :1])


def solution(mesh):
    split = Mesh(mesh.devices.reshape(8, 4, mesh.shape["head"]), ("ctx_0", "ctx_1", "head"))
    in_specs = (P(CTX, "head"), P(CTX, "head"), P(CTX, "head"), P(None, None, CTX_HEAD))
    out_specs = (P(CTX, "head"), P("head", CTX, None), P("head", None), P("head"))
    return jax.shard_map(
        on_device, mesh=split, in_specs=in_specs, out_specs=out_specs, check_vma=False
    )
```
